32 devices in a mesh: section: 1, dp: 32 (over z, y, x, core).
Axes of the slice: x: 2, y: 2, z: 4, core: 2. Of those that a mesh axis runs over, the one named last changes fastest.
Arguments:
- tokens: bfloat16 [4096, 8192], P('dp'), may hold values from -6 to 6
- blocks_in: bfloat16 [1, 160, 128, 128], P('section', 'dp'), may hold values from -0.078125 to 0.078125
- blocks_out: bfloat16 [1, 160, 128, 128], P('section', 'dp'), may hold values from -0.3125 to 0.3125
- pos_in: int32 [1, 160], P('section', 'dp'), may hold values from 0 to 256, as said below
- pos_out: int32 [1, 160], P('section', 'dp'), may hold values from 0 to 256, as said below
- cotangent: bfloat16 [4096, 8192], P('dp'), may hold values from -0.08984375 to 0.08984375
Outputs:
- grad_in: bfloat16 [1, 160, 128, 128], P('section', 'dp')
- grad_out: bfloat16 [1, 160, 128, 128], P('section', 'dp')
The draws below stay inside these ranges and needn't reach their ends.
Inputs may be any that keep to these rules, and one draw needn't show every extreme that they name: For each layer the first k slots (k from 110 to 160) hold distinct block numbers and the other slots hold 256, marking an empty slot; in each of pos_in and pos_out some layer fills all 160 slots. `pos_out`: as for pos_in, drawn independently.
All inputs are finite; a program needn't handle non-finite values.
Results may differ from the reference program's by a relative error of at most 0.023.
Values may be sent and summed in bfloat16 or wider, within the bound.
A program may use at most 128 MiB of HBM per device.

```python
import jax
import jax.numpy as jnp
from jax import lax

D = 8192
RANK = 512
BLOCK = 128
CAP = 160
LIVE_LO = 110
NBLK = 256
TOK_DEV = 128
LAYERS = 1
TOKENS = 4096
N_DP = 32


def block_places(key, which):
    base = jax.random.fold_in(key, 77)
    count_key = jax.random.fold_in(jax.random.fold_in(base, 1), which)
    full_key = jax.random.fold_in(jax.random.fold_in(base, 2), which)
    perm_key = jax.random.fold_in(jax.random.fold_in(base, 3), which)
    counts = jax.random.randint(count_key, (LAYERS,), LIVE_LO, CAP + 1)
    filled = jax.random.randint(full_key, (), 0, LAYERS)
    counts = jnp.where(jnp.arange(LAYERS) == filled, CAP, counts)
    layer_keys = jax.random.split(perm_key, LAYERS)
    perms = jax.vmap(lambda kk: jax.random.permutation(kk, NBLK)[:CAP])(layer_keys)
    slots = jnp.arange(CAP)
    return jnp.where(slots[None, :] < counts[:, None], perms, NBLK).astype(jnp.int32)


def draw_pos_in(key, part):
    return block_places(key, 0)


def draw_pos_out(key, part):
    return block_places(key, 1)


def block_levels(stream_key, dims, cuts, least, largest):
    gain = 1.0
    for dim, blocks in cuts:
        heights = jax.random.uniform(jax.random.fold_in(jax.random.fold_in(stream_key, 6), dim), (blocks,), jnp.float32, least / len(cuts), largest / len(cuts))
        gain = gain * jnp.repeat(jnp.exp(heights), dims[dim] // blocks).reshape((-1,) + (1,) * (len(dims) - 1 - dim))
    return gain


def centred(own_key, shape, deviation, limit, pieces=(), kind=jnp.bfloat16):
    values = deviation * jax.random.normal(own_key, shape, jnp.float32)
    if pieces:
        values = values * block_levels(own_key, shape, pieces, -0.22, 0.18)
    return jnp.clip(values, -limit, limit).astype(kind)


def setup_inputs(seed: int = 0) -> dict:
    key_list = jax.random.split(jax.random.key(seed), 7)
    return {
        "tokens": centred(key_list[0], (TOKENS, D), 1.0, 6.0, ((0, 32),)),
        "blocks_in": centred(key_list[1], (LAYERS, CAP, BLOCK, BLOCK), (CAP * BLOCK * BLOCK // RANK) ** -0.5, 0.078125, ((1, 32),)),
        "blocks_out": centred(key_list[2], (LAYERS, CAP, BLOCK, BLOCK), (CAP * BLOCK * BLOCK // D) ** -0.5, 0.3125, ((1, 32),)),
        "pos_in": draw_pos_in(jax.random.fold_in(key_list[6], 71), 0),
        "pos_out": draw_pos_out(jax.random.fold_in(key_list[6], 71), 0),
        "cotangent": centred(key_list[5], (TOKENS, D), 0.015625, 0.08984375, ((0, 32),)),
    }


EPS = 1e-05

def expand(blocks, places, rows_b, cols_b):
    flat = jnp.zeros((rows_b * cols_b, BLOCK, BLOCK), blocks.dtype)
    flat = flat.at[places].set(blocks, mode='drop')
    return flat.reshape(rows_b, cols_b, BLOCK, BLOCK).transpose(0, 2, 1, 3).reshape(rows_b * BLOCK, cols_b * BLOCK)

def pack(dense, places, rows_b, cols_b):
    blocks = dense.reshape(rows_b, BLOCK, cols_b, BLOCK).transpose(0, 2, 1, 3).reshape(rows_b * cols_b, BLOCK, BLOCK)
    return jnp.take(blocks, places, axis=0, mode='fill', fill_value=0.0)

def norm_parts(hidden):
    wide = hidden.astype(jnp.float32)
    scale = jnp.sqrt(lax.optimization_barrier(jnp.mean(wide * wide, axis=-1, keepdims=True)) + EPS)
    return (wide, scale)

def device_sums(left, right, places, rows_b, cols_b):
    left_dev = left.reshape(N_DP, TOK_DEV, left.shape[1])
    right_dev = right.reshape(N_DP, TOK_DEV, right.shape[1])

    def step(total, pair):
        part = lax.dot_general(pair[0], pair[1], (((0,), (0,)), ((), ())), preferred_element_type=jnp.float32)
        packed = pack(part, places, rows_b, cols_b).astype(jnp.bfloat16)
        packed = lax.optimization_barrier(packed)
        return (total + packed.astype(jnp.float32), None)
    init = jnp.zeros((places.shape[0], BLOCK, BLOCK), jnp.float32)
    total, _ = lax.scan(step, init, (left_dev, right_dev))
    return total

def reference(tokens, blocks_in, blocks_out, pos_in, pos_out, cotangent):
    rows_d = D // BLOCK
    rows_k = RANK // BLOCK
    mats_a = [expand(blocks_in[l], pos_in[l], rows_d, rows_k) for l in range(LAYERS)]
    mats_b = [expand(blocks_out[l], pos_out[l], rows_k, rows_d) for l in range(LAYERS)]
    states = [tokens]
    for l in range(LAYERS):
        wide, scale = norm_parts(states[l])
        normed = (wide / scale).astype(jnp.bfloat16)
        pre = jnp.dot(normed, mats_a[l], preferred_element_type=jnp.float32)
        act = (pre * jax.nn.sigmoid(pre)).astype(jnp.bfloat16)
        states.append((wide + jnp.dot(act, mats_b[l], preferred_element_type=jnp.float32)).astype(jnp.bfloat16))
    upstream = cotangent
    grads_in = [None] * LAYERS
    grads_out = [None] * LAYERS
    for l in reversed(range(LAYERS)):
        wide, scale = norm_parts(states[l])
        unit = wide / scale
        normed = unit.astype(jnp.bfloat16)
        pre = jnp.dot(normed, mats_a[l], preferred_element_type=jnp.float32)
        sig = jax.nn.sigmoid(pre)
        act = (pre * sig).astype(jnp.bfloat16)
        dact = lax.dot_general(upstream, mats_b[l], (((1,), (1,)), ((), ())), preferred_element_type=jnp.float32)
        dpre = (dact * sig * (1.0 + pre * (1.0 - sig))).astype(jnp.bfloat16)
        dnorm = lax.dot_general(dpre, mats_a[l], (((1,), (1,)), ((), ())), preferred_element_type=jnp.float32)
        grads_in[l] = device_sums(normed, dpre, pos_in[l], rows_d, rows_k).astype(jnp.bfloat16)
        grads_out[l] = device_sums(act, upstream, pos_out[l], rows_k, rows_d).astype(jnp.bfloat16)
        inner = lax.optimization_barrier(jnp.mean(dnorm * unit, axis=-1, keepdims=True))
        upstream = (upstream.astype(jnp.float32) + (dnorm - unit * inner) / scale).astype(jnp.bfloat16)
    return (jnp.stack(grads_in), jnp.stack(grads_out))
```

```python
import functools

import jax
import jax.numpy as jnp
from jax import lax
from jax.experimental import pallas as pl
from jax.experimental.pallas import tpu as pltpu
from jax.sharding import PartitionSpec as P

D = 8192
RANK = 512
BLOCK = 128
MICRO = 2


EPS = 1e-05


def from_behind(block, axis, distance):
    devices = range(lax.axis_size(axis))
    route = [(i - distance, i) for i in devices if i - distance in devices]
    return lax.ppermute(block, axis, route)


def expand(blocks, places, rows_b, cols_b):
    flat = jnp.zeros((rows_b * cols_b, BLOCK, BLOCK), blocks.dtype)
    flat = flat.at[places].set(blocks, mode="drop")
    return (
        flat.reshape(rows_b, cols_b, BLOCK, BLOCK)
        .transpose(0, 2, 1, 3)
        .reshape(rows_b * BLOCK, cols_b * BLOCK)
    )


def slot_grads(left, right, places, rows_b, cols_b):
    count = left.shape[0]
    valid = places < rows_b * cols_b
    row_block = jnp.where(valid, places // cols_b, 0).astype(jnp.int32)
    col_block = jnp.where(valid, places % cols_b, 0).astype(jnp.int32)
    left_blocks = jnp.take(left.reshape(count, rows_b, BLOCK), row_block, axis=1)
    right_blocks = jnp.take(right.reshape(count, cols_b, BLOCK), col_block, axis=1)
    result = jnp.einsum(
        "tjb,tjc->jbc", left_blocks, right_blocks, preferred_element_type=jnp.float32
    )
    return jnp.where(valid[:, None, None], result, 0.0)


def norm_parts(hidden):
    wide = hidden.astype(jnp.float32)
    scale = jnp.sqrt(jnp.mean(wide * wide, axis=-1, keepdims=True) + EPS)
    return (wide, scale)


def forward_layer(hidden, mat_a, mat_b):
    wide, scale = norm_parts(hidden)
    normed = (wide / scale).astype(jnp.bfloat16)
    pre = jnp.dot(normed, mat_a, preferred_element_type=jnp.float32)
    act = (pre * jax.nn.sigmoid(pre)).astype(jnp.bfloat16)
    return (wide + jnp.dot(act, mat_b, preferred_element_type=jnp.float32)).astype(jnp.bfloat16)


def backward_layer(hidden, upstream, mat_a, mat_b):
    wide, scale = norm_parts(hidden)
    unit = wide / scale
    normed = unit.astype(jnp.bfloat16)
    pre = jnp.dot(normed, mat_a, preferred_element_type=jnp.float32)
    sig = jax.nn.sigmoid(pre)
    act = (pre * sig).astype(jnp.bfloat16)
    dact = lax.dot_general(
        upstream, mat_b, (((1,), (1,)), ((), ())), preferred_element_type=jnp.float32
    )
    dpre = (dact * sig * (1.0 + pre * (1.0 - sig))).astype(jnp.bfloat16)
    dnorm = lax.dot_general(
        dpre, mat_a, (((1,), (1,)), ((), ())), preferred_element_type=jnp.float32
    )
    inner = jnp.mean(dnorm * unit, axis=-1, keepdims=True)
    earlier = (upstream.astype(jnp.float32) + (dnorm - unit * inner) / scale).astype(jnp.bfloat16)
    return (earlier, normed, dpre, act)


def store(stack, value, picked, active):
    updated = lax.dynamic_update_slice_in_dim(stack, value[None], picked, 0)
    return jnp.where(active, updated, stack)


def per_device(tokens, blocks_in, blocks_out, pos_in, pos_out, cotangent):
    sections = lax.axis_size("section")
    here = lax.axis_index("section")
    rows_d = D // BLOCK
    rows_k = RANK // BLOCK
    full_in, full_out, all_in, all_out = (
        lax.all_gather(blocks_in, "dp", axis=1, tiled=True),
        lax.all_gather(blocks_out, "dp", axis=1, tiled=True),
        lax.all_gather(pos_in, "dp", axis=1, tiled=True),
        lax.all_gather(pos_out, "dp", axis=1, tiled=True),
    )
    mat_a = expand(full_in[0], all_in[0], rows_d, rows_k)
    mat_b = expand(full_out[0], all_out[0], rows_k, rows_d)
    micro_rows = tokens.shape[0] // MICRO
    turns = MICRO + sections - 1
    saved = jnp.zeros((MICRO, micro_rows, D), jnp.bfloat16)
    carried = jnp.zeros((micro_rows, D), jnp.bfloat16)
    for turn in range(turns):
        micro = turn - here
        active = (micro >= 0) & (micro < MICRO)
        picked = jnp.clip(micro, 0, MICRO - 1)
        first = lax.dynamic_slice_in_dim(tokens, picked * micro_rows, micro_rows, 0)
        entering = jnp.where(here == 0, first, carried)
        saved = store(saved, entering, picked, active)
        if turn < turns - 1:
            leaving = lax.cond(
                active, lambda x: forward_layer(x, mat_a, mat_b), lambda x: x, entering
            )
            carried = from_behind(leaving, "section", 1)
    kept_normed = jnp.zeros((MICRO, micro_rows, D), jnp.bfloat16)
    kept_dpre = jnp.zeros((MICRO, micro_rows, RANK), jnp.bfloat16)
    kept_act = jnp.zeros((MICRO, micro_rows, RANK), jnp.bfloat16)
    kept_upper = jnp.zeros((MICRO, micro_rows, D), jnp.bfloat16)
    carried_grad = jnp.zeros((micro_rows, D), jnp.bfloat16)
    for turn in range(turns):
        micro = turn - (sections - 1 - here)
        active = (micro >= 0) & (micro < MICRO)
        picked = jnp.clip(micro, 0, MICRO - 1)
        last = lax.dynamic_slice_in_dim(cotangent, picked * micro_rows, micro_rows, 0)
        upstream = jnp.where(here == sections - 1, last, carried_grad)
        hidden = lax.dynamic_index_in_dim(saved, picked, 0, keepdims=False)

        def run_layer():
            return backward_layer(hidden, upstream, mat_a, mat_b)

        def skip_layer():
            return (
                upstream,
                jnp.zeros((micro_rows, D), jnp.bfloat16),
                jnp.zeros((micro_rows, RANK), jnp.bfloat16),
                jnp.zeros((micro_rows, RANK), jnp.bfloat16),
            )

        earlier, normed, dpre, act = lax.cond(active, run_layer, skip_layer)
        kept_normed = store(kept_normed, normed, picked, active)
        kept_dpre = store(kept_dpre, dpre, picked, active)
        kept_act = store(kept_act, act, picked, active)
        kept_upper = store(kept_upper, upstream, picked, active)
        if turn < turns - 1:
            carried_grad = from_behind(earlier, "section", -1)
    all_rows = MICRO * micro_rows
    terms_in = slot_grads(
        kept_normed.reshape(all_rows, D),
        kept_dpre.reshape(all_rows, RANK),
        all_in[0],
        rows_d,
        rows_k,
    )[None]
    terms_out = slot_grads(
        kept_act.reshape(all_rows, RANK),
        kept_upper.reshape(all_rows, D),
        all_out[0],
        rows_k,
        rows_d,
    )[None]
    sums_in, sums_out = (
        lax.psum_scatter(
            terms_in.astype(jnp.bfloat16), "dp", scatter_dimension=1, tiled=True
        ).astype(jnp.float32),
        lax.psum_scatter(
            terms_out.astype(jnp.bfloat16), "dp", scatter_dimension=1, tiled=True
        ).astype(jnp.float32),
    )
    return (sums_in.astype(jnp.bfloat16), sums_out.astype(jnp.bfloat16))


EXTRA= 16
WIDE = 1024


class Place:
    def __init__(self, devices):
        me = lax.axis_index("dp")
        self.depth = devices // 8
        self.me = me
        self.core = me % 2
        self.chip = me // 2
        x = self.chip % 2
        y = (self.chip // 2) % 2
        self.z = self.chip // 4
        dx = 1 - 2 * x
        dy = 2 * (1 - 2 * y)
        self.first = (1 - self.core) * dx + self.core * dy
        self.second = (1 - self.core) * dy + self.core * dx
        self.sibling = me + 1 - 2 * self.core

    def member(self, ds, df, dz, first=None, second=None):
        first = self.first if first is None else first
        second = self.second if second is None else second
        along = ((self.z + dz) % self.depth - self.z) * 4
        return self.chip + along + df * first + ds * second

    def device(self, ds, df, dz):
        return 2 * self.member(ds, df, dz) + self.core

    def greet(self):
        peers = [self.sibling, self.device(1, 0, 0), self.device(0, 1, 0)]
        peers += [self.device(0, 0, d) for d in range(1, self.depth)]
        barrier = pltpu.get_barrier_semaphore()
        for peer in peers:
            pl.semaphore_signal(
                barrier, inc=1, device_id={"dp": peer}, device_id_type=pl.DeviceIdType.MESH
            )
        pl.semaphore_wait(barrier, len(peers))


def remote(src, dst, send, recv, peer):
    return pltpu.make_async_remote_copy(
        src_ref=src,
        dst_ref=dst,
        send_sem=send,
        recv_sem=recv,
        device_id={"dp": peer},
        device_id_type=pl.DeviceIdType.MESH,
    )


def gather_kernel(devices, own, full, send_sems, chip_sems, sib_sems, pair_sems, copy_sems):
    at = Place(devices)
    depth = at.depth
    mine = at.core
    sends = []
    pair = []
    local = []
    for m in range(2):
        local.append(pltpu.make_async_copy(own.at[m], full.at[m, at.me], copy_sems.at[m]))
        local[-1].start()
    at.greet()

    def start(src, dst, recv, peer):
        copy = remote(src, dst, send_sems.at[len(sends)], recv, peer)
        copy.start()
        sends.append(copy)
        return copy

    for m in range(2):
        pair.append(start(own.at[m], full.at[m, at.me], pair_sems.at[m], at.sibling))

    def shard(chip):
        return full.at[mine, pl.ds(2 * chip, 2)]

    def push(chip, peer):
        start(shard(chip), shard(chip), chip_sems.at[chip], peer)

    def share(chip):
        start(shard(chip), shard(chip), sib_sems.at[chip], at.sibling)

    def arrived(chip):
        remote(shard(chip), shard(chip), send_sems.at[0], chip_sems.at[chip], at.sibling).wait_recv()

    first, second = at.device(0, 1, 0), at.device(1, 0, 0)
    for copy in local:
        copy.wait()
    for copy in pair:
        copy.wait_recv()
    here = at.chip
    order = list(range(1, depth))
    order = sorted(order, key=lambda d: (min(d, depth - d), d))
    push(here, second)
    push(here, first)
    for d in order:
        push(here, at.device(0, 0, d))
    for d in [0] + order:
        if d:
            chip = at.member(0, 0, d)
            arrived(chip)
            push(chip, first)
            push(chip, second)
            share(chip)
        chip = at.member(0, 1, d)
        arrived(chip)
        push(chip, second)
        share(chip)
    for df in range(2):
        for d in [0] + order:
            chip = at.member(1, df, d)
            arrived(chip)
            share(chip)
    for df in range(2):
        for ds in range(2):
            for d in range(depth):
                if df or ds or d:
                    chip = at.member(ds, df, d)
                    other = full.at[1 - mine, pl.ds(2 * chip, 2)]
                    remote(other, other, send_sems.at[0], sib_sems.at[chip], at.sibling).wait_recv()
    for copy in sends:
        copy.wait_send()


def gather_blocks(own, devices):
    chips = devices // 2
    depth = devices // 8
    sends = 2 + 2 + (depth - 1) + 3 * (depth - 1) + 2 * depth + 2 * depth
    return pl.pallas_call(
        functools.partial(gather_kernel, devices),
        out_shape=jax.ShapeDtypeStruct((2, devices) + own.shape[1:], own.dtype),
        in_specs=[pl.BlockSpec(memory_space=pltpu.VMEM)],
        out_specs=pl.BlockSpec(memory_space=pl.ANY),
        scratch_shapes=[
            pltpu.SemaphoreType.DMA((sends,)),
            pltpu.SemaphoreType.DMA((chips,)),
            pltpu.SemaphoreType.DMA((chips,)),
            pltpu.SemaphoreType.DMA((2,)),
            pltpu.SemaphoreType.DMA((2,)),
        ],
        compiler_params=pltpu.CompilerParams(collective_id=0, has_side_effects=True),
        name="gather_blocks",
    )(own)


def layer_kernel(per, pos, tokens, upper, full, out, mat_a, mat_b, normed):
    count, width = tokens.shape
    rank = mat_a.shape[1]
    devices = full.shape[1]
    rows_k = rank // BLOCK
    rows_d = width // BLOCK
    chunks = [slice(i, i + WIDE) for i in range(0, width, WIDE)]

    def wipe_a(i, carry):
        mat_a[pl.ds(pl.multiple_of(i * BLOCK, BLOCK), BLOCK), :] = jnp.zeros((BLOCK, rank), jnp.bfloat16)
        return carry

    lax.fori_loop(0, rows_d, wipe_a, 0)

    def wipe_b(i, carry):
        mat_b[:, pl.ds(pl.multiple_of(i * BLOCK, BLOCK), BLOCK)] = jnp.zeros(
            (mat_b.shape[0], BLOCK), jnp.bfloat16
        )
        return carry

    lax.fori_loop(0, rows_d, wipe_b, 0)

    def spot_a(j):
        p = pos[0, j]
        return (
            pl.ds(pl.multiple_of((p // rows_k) * BLOCK, BLOCK), BLOCK),
            pl.ds(pl.multiple_of((p % rows_k) * BLOCK, BLOCK), BLOCK),
        )

    def spot_b(j):
        p = pos[1, j]
        return (
            pl.ds(pl.multiple_of((p // rows_d) * BLOCK, BLOCK), BLOCK),
            pl.ds(pl.multiple_of((p % rows_d) * BLOCK, BLOCK), BLOCK),
        )

    def place(dev, carry):
        for i in range(per):
            rows = pl.ds(i * BLOCK, BLOCK)
            r, c = spot_a(dev * per + i)
            mat_a[r, c] = full[0, dev, rows, :]
            r, c = spot_b(dev * per + i)
            mat_b[r, c] = full[1, dev, rows, :]
        return carry

    lax.fori_loop(0, devices, place, 0)

    total = jnp.zeros((count, BLOCK), jnp.float32)
    for k in range(0, width, BLOCK):
        wide = tokens[:, k : k + BLOCK].astype(jnp.float32)
        total += wide * wide
    scale = jnp.sqrt(jnp.sum(total, axis=-1, keepdims=True) / width + EPS)
    inverse = 1.0 / scale
    pre = jnp.zeros((count, rank), jnp.float32)
    dact = jnp.zeros((count, rank), jnp.float32)
    for k in chunks:
        unit = (tokens[:, k].astype(jnp.float32) * inverse).astype(jnp.bfloat16)
        normed[:, k] = unit
        pre += jnp.dot(unit, mat_a[k, :], preferred_element_type=jnp.float32)
        dact += lax.dot_general(
            upper[:, k], mat_b[:rank, k], (((1,), (1,)), ((), ())), preferred_element_type=jnp.float32
        )
    sig = jax.nn.sigmoid(pre)
    act = (pre * sig).astype(jnp.bfloat16)
    dpre = (dact * sig * (1.0 + pre * (1.0 - sig))).astype(jnp.bfloat16)
    across = (((0,), (0,)), ((), ()))
    mat_a[width:, :] = jnp.zeros((BLOCK, rank), jnp.bfloat16)
    mat_b[rank:, :] = jnp.zeros((BLOCK, width), jnp.bfloat16)
    for k in chunks:
        mat_a[k, :] = lax.dot_general(
            normed[:, k], dpre, across, preferred_element_type=jnp.float32
        ).astype(jnp.bfloat16)
        mat_b[:rank, k] = lax.dot_general(
            act, upper[:, k], across, preferred_element_type=jnp.float32
        ).astype(jnp.bfloat16)

    def pick(dev, carry):
        for i in range(per):
            rows = pl.ds(i * BLOCK, BLOCK)
            r, c = spot_a(dev * per + i)
            out[0, dev, rows, :] = mat_a[r, c]
            r, c = spot_b(dev * per + i)
            out[1, dev, rows, :] = mat_b[r, c]
        return carry

    lax.fori_loop(0, devices, pick, 0)


def layer_terms(places, tokens, upper, full, per):
    count, width = tokens.shape
    devices = full.shape[1]
    vmem = pl.BlockSpec(memory_space=pltpu.VMEM)
    return pl.pallas_call(
        functools.partial(layer_kernel, per),
        out_shape=jax.ShapeDtypeStruct((2, devices, per * BLOCK, BLOCK), jnp.bfloat16),
        in_specs=[pl.BlockSpec(memory_space=pltpu.SMEM), vmem, vmem, vmem],
        out_specs=vmem,
        scratch_shapes=[
            pltpu.VMEM((width + BLOCK, RANK), jnp.bfloat16),
            pltpu.VMEM((RANK + BLOCK, width), jnp.bfloat16),
            pltpu.VMEM((count, width), jnp.bfloat16),
        ],
        compiler_params=pltpu.CompilerParams(vmem_limit_bytes=60 * 1024 * 1024),
        name="layer_terms",
    )(places, tokens, upper, full)


def scatter_kernel(devices, terms, out, held, final, pair_got, second_got, first_got, line_got, last_got,
                   load_sems, send_sems, pair_sems, second_sems, first_sems, line_sems, last_sem):
    at = Place(devices)
    depth = at.depth
    mine = at.core
    sends = []
    line = [0] + sorted(range(1, depth), key=lambda d: (min(d, depth - d), d))
    far = line[1:][::-1]
    order = [(1, 1, d) for d in far + [0]] + [(1, 0, d) for d in far + [0]]
    order += [(0, 1, d) for d in far + [0]] + [(0, 0, d) for d in far + [0]]
    loads = []
    for i, (ds, df, dz) in enumerate(order):
        chip = at.member(ds, df, dz)
        load = pltpu.make_async_copy(terms.at[mine, pl.ds(2 * chip, 2)], held.at[i], load_sems.at[i])
        load.start()
        loads.append(load)
    at.greet()

    def start(src, dst, recv, peer):
        copy = remote(src, dst, send_sems.at[len(sends)], recv, peer)
        copy.start()
        sends.append(copy)
        return copy

    pairs = []
    for i, (ds, df, dz) in enumerate(order):
        chip = at.member(ds, df, dz, at.second, at.first)
        pairs.append(
            start(terms.at[1 - mine, pl.ds(2 * chip, 2)], pair_got.at[i], pair_sems.at[i], at.sibling)
        )

    def got(buf, sem):
        remote(buf, buf, send_sems.at[0], sem, at.sibling).wait_recv()

    for i, (ds, df, dz) in enumerate(order):
        loads[i].wait()
        parts = [pair_got.at[i]]
        pairs[i].wait_recv()
        if not ds:
            parts.append(second_got.at[df * depth + dz])
            got(parts[-1], second_sems.at[df * depth + dz])
        if not ds and not df:
            parts.append(first_got.at[dz])
            got(parts[-1], first_sems.at[dz])
            if not dz:
                for d in range(1, depth):
                    parts.append(line_got.at[d - 1])
                    got(parts[-1], line_sems.at[d - 1])
        rows = held.shape[2]

        def add(step, carry, i=i, parts=parts):
            part = pl.ds(pl.multiple_of(step * BLOCK, BLOCK), BLOCK)
            for half in range(2):
                value = held[i, half, part, :].astype(jnp.float32)
                for p in parts:
                    value += p[half, part, :].astype(jnp.float32)
                held[i, half, part, :] = value.astype(jnp.bfloat16)
            return carry

        lax.fori_loop(0, rows // BLOCK, add, 0)
        if ds:
            start(held.at[i], second_got.at[df * depth + dz], second_sems.at[df * depth + dz], at.device(1, 0, 0))
        elif df:
            start(held.at[i], first_got.at[dz], first_sems.at[dz], at.device(0, 1, 0))
        elif dz:
            start(held.at[i], line_got.at[dz - 1], line_sems.at[dz - 1], at.device(0, 0, dz))
        else:
            last = start(held.at[i, 1 - mine], last_got, last_sem, at.sibling)
            final[...] = held[i, mine]
            last.wait_recv()
    out[mine] = final[...]
    out[1 - mine] = last_got[...]
    for copy in sends:
        copy.wait_send()


def scatter_terms(terms, devices):
    chips = devices // 2
    depth = devices // 8
    rows = terms.shape[2]
    shard = (2, rows, BLOCK)
    dma = pltpu.SemaphoreType.DMA
    return pl.pallas_call(
        functools.partial(scatter_kernel, devices),
        out_shape=jax.ShapeDtypeStruct(shard, jnp.bfloat16),
        in_specs=[pl.BlockSpec(memory_space=pl.ANY)],
        out_specs=pl.BlockSpec(memory_space=pltpu.VMEM),
        scratch_shapes=[
            pltpu.VMEM((chips,) + shard, jnp.bfloat16),
            pltpu.VMEM((rows, BLOCK), jnp.bfloat16),
            pltpu.VMEM((chips,) + shard, jnp.bfloat16),
            pltpu.VMEM((2 * depth,) + shard, jnp.bfloat16),
            pltpu.VMEM((depth,) + shard, jnp.bfloat16),
            pltpu.VMEM((depth - 1,) + shard, jnp.bfloat16),
            pltpu.VMEM((rows, BLOCK), jnp.bfloat16),
            dma((chips,)),
            dma((2 * chips,)),
            dma((chips,)),
            dma((2 * depth,)),
            dma((depth,)),
            dma((depth - 1,)),
            dma,
        ],
        compiler_params=pltpu.CompilerParams(collective_id=1, has_side_effects=True),
        name="scatter_terms",
    )(terms)


def one_section(tokens, blocks_in, blocks_out, pos_in, pos_out, cotangent):
    devices = lax.axis_size("dp")
    per = blocks_in.shape[1]
    blocks = jnp.stack([blocks_in[0], blocks_out[0]]).reshape(2, per * BLOCK, BLOCK)
    places = jnp.concatenate([pos_in, pos_out]).astype(jnp.bfloat16)
    places = jnp.pad(places[:, None, :], ((0, 0), (0, EXTRA - 1), (0, BLOCK - per)))
    full = gather_blocks(jnp.concatenate([blocks, places], axis=1), devices)
    everywhere = full[:, :, per * BLOCK, :per].astype(jnp.int32).reshape(2, devices * per)
    terms = layer_terms(everywhere, tokens, cotangent, full, per)
    sums = scatter_terms(terms, devices)
    shape = blocks_in.shape
    return (sums[0].reshape(shape), sums[1].reshape(shape))


def solution(mesh):
    in_specs = (
        P("dp", None),
        P("section", "dp", None, None),
        P("section", "dp", None, None),
        P("section", "dp"),
        P("section", "dp"),
        P("dp", None),
    )
    out_specs = (P("section", "dp", None, None), P("section", "dp", None, None))
    body = one_section if mesh.shape["section"] == 1 else per_device
    return jax.shard_map(
        body, mesh=mesh, in_specs=in_specs, out_specs=out_specs, check_vma=False
    )
```

```python
import functools

import jax
import jax.numpy as jnp
from jax import lax
from jax.experimental import pallas as pl
from jax.experimental.pallas import tpu as pltpu
from jax.sharding import PartitionSpec as P

D = 8192
RANK = 512
BLOCK = 128
MICRO = 2


EPS = 1e-05


def from_behind(block, axis, distance):
    devices = range(lax.axis_size(axis))
    route = [(i - distance, i) for i in devices if i - distance in devices]
    return lax.ppermute(block, axis, route)


def expand(blocks, places, rows_b, cols_b):
    flat = jnp.zeros((rows_b * cols_b, BLOCK, BLOCK), blocks.dtype)
    flat = flat.at[places].set(blocks, mode="drop")
    return (
        flat.reshape(rows_b, cols_b, BLOCK, BLOCK)
        .transpose(0, 2, 1, 3)
        .reshape(rows_b * BLOCK, cols_b * BLOCK)
    )


def slot_grads(left, right, places, rows_b, cols_b):
    count = left.shape[0]
    valid = places < rows_b * cols_b
    row_block = jnp.where(valid, places // cols_b, 0).astype(jnp.int32)
    col_block = jnp.where(valid, places % cols_b, 0).astype(jnp.int32)
    left_blocks = jnp.take(left.reshape(count, rows_b, BLOCK), row_block, axis=1)
    right_blocks = jnp.take(right.reshape(count, cols_b, BLOCK), col_block, axis=1)
    result = jnp.einsum(
        "tjb,tjc->jbc", left_blocks, right_blocks, preferred_element_type=jnp.float32
    )
    return jnp.where(valid[:, None, None], result, 0.0)


def norm_parts(hidden):
    wide = hidden.astype(jnp.float32)
    scale = jnp.sqrt(jnp.mean(wide * wide, axis=-1, keepdims=True) + EPS)
    return (wide, scale)


def forward_layer(hidden, mat_a, mat_b):
    wide, scale = norm_parts(hidden)
    normed = (wide / scale).astype(jnp.bfloat16)
    pre = jnp.dot(normed, mat_a, preferred_element_type=jnp.float32)
    act = (pre * jax.nn.sigmoid(pre)).astype(jnp.bfloat16)
    return (wide + jnp.dot(act, mat_b, preferred_element_type=jnp.float32)).astype(jnp.bfloat16)


def backward_layer(hidden, upstream, mat_a, mat_b):
    wide, scale = norm_parts(hidden)
    unit = wide / scale
    normed = unit.astype(jnp.bfloat16)
    pre = jnp.dot(normed, mat_a, preferred_element_type=jnp.float32)
    sig = jax.nn.sigmoid(pre)
    act = (pre * sig).astype(jnp.bfloat16)
    dact = lax.dot_general(
        upstream, mat_b, (((1,), (1,)), ((), ())), preferred_element_type=jnp.float32
    )
    dpre = (dact * sig * (1.0 + pre * (1.0 - sig))).astype(jnp.bfloat16)
    dnorm = lax.dot_general(
        dpre, mat_a, (((1,), (1,)), ((), ())), preferred_element_type=jnp.float32
    )
    inner = jnp.mean(dnorm * unit, axis=-1, keepdims=True)
    earlier = (upstream.astype(jnp.float32) + (dnorm - unit * inner) / scale).astype(jnp.bfloat16)
    return (earlier, normed, dpre, act)


def store(stack, value, picked, active):
    updated = lax.dynamic_update_slice_in_dim(stack, value[None], picked, 0)
    return jnp.where(active, updated, stack)


def per_device(tokens, blocks_in, blocks_out, pos_in, pos_out, cotangent):
    sections = lax.axis_size("section")
    here = lax.axis_index("section")
    rows_d = D // BLOCK
    rows_k = RANK // BLOCK
    full_in, full_out, all_in, all_out = (
        lax.all_gather(blocks_in, "dp", axis=1, tiled=True),
        lax.all_gather(blocks_out, "dp", axis=1, tiled=True),
        lax.all_gather(pos_in, "dp", axis=1, tiled=True),
        lax.all_gather(pos_out, "dp", axis=1, tiled=True),
    )
    mat_a = expand(full_in[0], all_in[0], rows_d, rows_k)
    mat_b = expand(full_out[0], all_out[0], rows_k, rows_d)
    micro_rows = tokens.shape[0] // MICRO
    turns = MICRO + sections - 1
    saved = jnp.zeros((MICRO, micro_rows, D), jnp.bfloat16)
    carried = jnp.zeros((micro_rows, D), jnp.bfloat16)
    for turn in range(turns):
        micro = turn - here
        active = (micro >= 0) & (micro < MICRO)
        picked = jnp.clip(micro, 0, MICRO - 1)
        first = lax.dynamic_slice_in_dim(tokens, picked * micro_rows, micro_rows, 0)
        entering = jnp.where(here == 0, first, carried)
        saved = store(saved, entering, picked, active)
        if turn < turns - 1:
            leaving = lax.cond(
                active, lambda x: forward_layer(x, mat_a, mat_b), lambda x: x, entering
            )
            carried = from_behind(leaving, "section", 1)
    kept_normed = jnp.zeros((MICRO, micro_rows, D), jnp.bfloat16)
    kept_dpre = jnp.zeros((MICRO, micro_rows, RANK), jnp.bfloat16)
    kept_act = jnp.zeros((MICRO, micro_rows, RANK), jnp.bfloat16)
    kept_upper = jnp.zeros((MICRO, micro_rows, D), jnp.bfloat16)
    carried_grad = jnp.zeros((micro_rows, D), jnp.bfloat16)
    for turn in range(turns):
        micro = turn - (sections - 1 - here)
        active = (micro >= 0) & (micro < MICRO)
        picked = jnp.clip(micro, 0, MICRO - 1)
        last = lax.dynamic_slice_in_dim(cotangent, picked * micro_rows, micro_rows, 0)
        upstream = jnp.where(here == sections - 1, last, carried_grad)
        hidden = lax.dynamic_index_in_dim(saved, picked, 0, keepdims=False)

        def run_layer():
            return backward_layer(hidden, upstream, mat_a, mat_b)

        def skip_layer():
            return (
                upstream,
                jnp.zeros((micro_rows, D), jnp.bfloat16),
                jnp.zeros((micro_rows, RANK), jnp.bfloat16),
                jnp.zeros((micro_rows, RANK), jnp.bfloat16),
            )

        earlier, normed, dpre, act = lax.cond(active, run_layer, skip_layer)
        kept_normed = store(kept_normed, normed, picked, active)
        kept_dpre = store(kept_dpre, dpre, picked, active)
        kept_act = store(kept_act, act, picked, active)
        kept_upper = store(kept_upper, upstream, picked, active)
        if turn < turns - 1:
            carried_grad = from_behind(earlier, "section", -1)
    all_rows = MICRO * micro_rows
    terms_in = slot_grads(
        kept_normed.reshape(all_rows, D),
        kept_dpre.reshape(all_rows, RANK),
        all_in[0],
        rows_d,
        rows_k,
    )[None]
    terms_out = slot_grads(
        kept_act.reshape(all_rows, RANK),
        kept_upper.reshape(all_rows, D),
        all_out[0],
        rows_k,
        rows_d,
    )[None]
    sums_in, sums_out = (
        lax.psum_scatter(
            terms_in.astype(jnp.bfloat16), "dp", scatter_dimension=1, tiled=True
        ).astype(jnp.float32),
        lax.psum_scatter(
            terms_out.astype(jnp.bfloat16), "dp", scatter_dimension=1, tiled=True
        ).astype(jnp.float32),
    )
    return (sums_in.astype(jnp.bfloat16), sums_out.astype(jnp.bfloat16))


EXTRA= 16
WIDE = 1024


class Place:
    def __init__(self, devices):
        me = lax.axis_index("dp")
        self.depth = devices // 8
        self.me = me
        self.core = me % 2
        self.chip = me // 2
        x = self.chip % 2
        y = (self.chip // 2) % 2
        self.z = self.chip // 4
        dx = 1 - 2 * x
        dy = 2 * (1 - 2 * y)
        self.first = (1 - self.core) * dx + self.core * dy
        self.second = (1 - self.core) * dy + self.core * dx
        self.sibling = me + 1 - 2 * self.core

    def member(self, ds, df, dz, first=None, second=None):
        first = self.first if first is None else first
        second = self.second if second is None else second
        along = ((self.z + dz) % self.depth - self.z) * 4
        return self.chip + along + df * first + ds * second

    def device(self, ds, df, dz):
        return 2 * self.member(ds, df, dz) + self.core

    def knock(self):
        peers = [self.sibling, self.device(1, 0, 0), self.device(0, 1, 0)]
        peers += [self.device(0, 0, d) for d in range(1, self.depth)]
        barrier = pltpu.get_barrier_semaphore()
        for peer in peers:
            pl.semaphore_signal(
                barrier, inc=1, device_id={"dp": peer}, device_id_type=pl.DeviceIdType.MESH
            )
        return lambda: pl.semaphore_wait(barrier, len(peers))


def remote(src, dst, send, recv, peer):
    return pltpu.make_async_remote_copy(
        src_ref=src,
        dst_ref=dst,
        send_sem=send,
        recv_sem=recv,
        device_id={"dp": peer},
        device_id_type=pl.DeviceIdType.MESH,
    )


def gather_kernel(devices, own, own_tags, tokens, cotangent, full, tags, other, send_sems, chip_sems, misc_sems):
    at = Place(devices)
    depth = at.depth
    mine = at.core
    sends = []
    local = [
        pltpu.make_async_copy(own.at[mine], full.at[at.me], misc_sems.at[0]),
        pltpu.make_async_copy(own_tags.at[mine], tags.at[at.me], misc_sems.at[3]),
    ]
    for copy in local:
        copy.start()
    at.knock()()

    def start(src, dst, recv, peer):
        copy = remote(src, dst, send_sems.at[len(sends)], recv, peer)
        copy.start()
        sends.append(copy)
        return copy

    pair = [
        start(own.at[1 - mine], full.at[at.me], misc_sems.at[1], at.sibling),
        start(own_tags.at[1 - mine], tags.at[at.me], misc_sems.at[4], at.sibling),
    ]

    def shards(chip):
        return ((full.at[pl.ds(2 * chip, 2)], chip_sems.at[0, chip]), (tags.at[pl.ds(2 * chip, 2)], chip_sems.at[1, chip]))

    def push(chip, peer):
        for shard, sem in shards(chip):
            start(shard, shard, sem, peer)

    def arrived(chip):
        for shard, sem in shards(chip):
            remote(shard, shard, send_sems.at[0], sem, at.sibling).wait_recv()

    first, second = at.device(0, 1, 0), at.device(1, 0, 0)
    for copy in local:
        copy.wait()
    for copy in pair:
        copy.wait_recv()
    here = at.chip
    order = list(range(1, depth))
    order = sorted(order, key=lambda d: (min(d, depth - d), d))
    push(here, second)
    push(here, first)
    for d in order:
        push(here, at.device(0, 0, d))
    give = remote(tokens, other, send_sems.at[len(sends)], misc_sems.at[2], at.sibling)

    @pl.when(mine == 0)
    def _():
        remote(cotangent, other, send_sems.at[len(sends)], misc_sems.at[2], at.sibling).start()

    @pl.when(mine == 1)
    def _():
        give.start()

    sends.append(give)
    for d in [0] + order:
        if d:
            chip = at.member(0, 0, d)
            arrived(chip)
            push(chip, first)
            push(chip, second)
        chip = at.member(0, 1, d)
        arrived(chip)
        push(chip, second)
    for df in range(2):
        for d in [0] + order:
            arrived(at.member(1, df, d))
    give.wait_recv()
    for copy in sends:
        copy.wait_send()


def gather_blocks(own, own_tags, tokens, cotangent, devices):
    chips = devices // 2
    depth = devices // 8
    sends = 2 * (1 + 2 + (depth - 1) + 2 * (depth - 1) + depth) + 1
    anywhere = pl.BlockSpec(memory_space=pl.ANY)
    return pl.pallas_call(
        functools.partial(gather_kernel, devices),
        out_shape=(
            jax.ShapeDtypeStruct((devices,) + own.shape[1:], own.dtype),
            jax.ShapeDtypeStruct((devices,) + own_tags.shape[1:], own_tags.dtype),
            jax.ShapeDtypeStruct(tokens.shape, tokens.dtype),
        ),
        in_specs=[pl.BlockSpec(memory_space=pltpu.VMEM)] * 2 + [anywhere, anywhere],
        out_specs=(anywhere, anywhere, anywhere),
        scratch_shapes=[
            pltpu.SemaphoreType.DMA((sends,)),
            pltpu.SemaphoreType.DMA((2, chips)),
            pltpu.SemaphoreType.DMA((5,)),
        ],
        compiler_params=pltpu.CompilerParams(collective_id=0, has_side_effects=True),
        name="gather_blocks",
    )(own, own_tags, tokens, cotangent)


def layer_kernel(devices, per, pos, begin, tokens, cotangent, other, full, out,
                 blocks, rows, mat_a, mat_b, grads, middle, middle_got, inverse,
                 held, second_got, first_got, line_got, last_got,
                 load_sems, send_sems, second_sems, first_sems, line_sems, pair_sems):
    at = Place(devices)
    depth = at.depth
    mine = at.core
    count, width = tokens.shape
    rank = mat_a.shape[1]
    rows_k = rank // BLOCK
    rows_d = width // BLOCK
    chunks = [slice(i, i + WIDE) for i in range(0, width, WIDE)]
    sends = []

    def start(src, dst, recv, peer):
        copy = remote(src, dst, send_sems.at[len(sends)], recv, peer)
        copy.start()
        sends.append(copy)
        return copy

    def got(buf, sem):
        remote(buf, buf, send_sems.at[0], sem, at.sibling).wait_recv()

    used = full.shape[0]
    load_blocks = pltpu.make_async_copy(full, blocks.at[pl.ds(0, used)], load_sems.at[0])
    load_blocks.start()
    load_own = pltpu.make_async_copy(tokens, rows.at[pl.ds(mine * count, count)], load_sems.at[1])

    @pl.when(mine == 0)
    def _():
        load_own.start()

    @pl.when(mine == 1)
    def _():
        pltpu.make_async_copy(cotangent, rows.at[pl.ds(mine * count, count)], load_sems.at[1]).start()

    load_other = pltpu.make_async_copy(other, rows.at[pl.ds((1 - mine) * count, count)], load_sems.at[2])
    load_other.start()
    wait_peers = at.knock()
    blocks[used] = jnp.zeros((BLOCK, BLOCK), jnp.bfloat16)
    grads[rows_d * rows_k] = jnp.zeros((BLOCK, BLOCK), jnp.bfloat16)
    load_blocks.wait()

    def slot_of(b):
        return blocks[begin[b]]

    @pl.when(mine == 0)
    def _():
        def expand_a(r, carry):
            into = pl.ds(pl.multiple_of(r * BLOCK, BLOCK), BLOCK)
            for c in range(rows_k):
                mat_a[into, c * BLOCK : (c + 1) * BLOCK] = slot_of(r * rows_k + c)
            return carry

        lax.fori_loop(0, rows_d, expand_a, 0)

    @pl.when(mine == 1)
    def _():
        def expand_b(c, carry):
            into = pl.ds(pl.multiple_of(c * BLOCK, BLOCK), BLOCK)
            for r in range(rows_k):
                mat_b[r * BLOCK : (r + 1) * BLOCK, into] = slot_of(r * rows_d + c)
            return carry

        lax.fori_loop(0, rows_d, expand_b, 0)

    load_own.wait()
    load_other.wait()

    @pl.when(mine == 0)
    def _():
        total = jnp.zeros((2 * count, BLOCK), jnp.float32)
        for k in range(0, width, BLOCK):
            wide = rows[:, k : k + BLOCK].astype(jnp.float32)
            total += wide * wide
        scale = jnp.sqrt(jnp.sum(total, axis=-1, keepdims=True) / width + EPS)
        inverse[...] = jnp.broadcast_to(1.0 / scale, inverse.shape)
        pre = jnp.zeros((2 * count, rank), jnp.float32)
        for k in chunks:
            pre += jnp.dot(rows[:, k], mat_a[k, :], preferred_element_type=jnp.float32)
        middle[...] = pre * inverse[:, :1]

    @pl.when(mine == 1)
    def _():
        dact = jnp.zeros((2 * count, rank), jnp.float32)
        for k in chunks:
            dact += lax.dot_general(
                rows[:, k], mat_b[:, k], (((1,), (1,)), ((), ())), preferred_element_type=jnp.float32
            )
        middle[...] = dact

    wait_peers()
    start(middle, middle_got, pair_sems.at[0], at.sibling).wait_recv()
    across = (((0,), (0,)), ((), ()))

    @pl.when(mine == 0)
    def _():
        pre = middle[...]
        sig = jax.nn.sigmoid(pre)
        dpre = middle_got[...] * sig * (1.0 + pre * (1.0 - sig))
        dpre = (dpre * inverse[:, :1]).astype(jnp.bfloat16)
        for k in chunks:
            part = lax.dot_general(
                rows[:, k], dpre, across, preferred_element_type=jnp.float32
            ).astype(jnp.bfloat16)
            for r in range(WIDE // BLOCK):
                for c in range(rows_k):
                    grads[(k.start // BLOCK + r) * rows_k + c] = part[
                        r * BLOCK : (r + 1) * BLOCK, c * BLOCK : (c + 1) * BLOCK
                    ]

    @pl.when(mine == 1)
    def _():
        pre = middle_got[...]
        act = (pre * jax.nn.sigmoid(pre)).astype(jnp.bfloat16)
        for k in chunks:
            part = lax.dot_general(
                act, rows[:, k], across, preferred_element_type=jnp.float32
            ).astype(jnp.bfloat16)
            for r in range(rows_k):
                for c in range(WIDE // BLOCK):
                    grads[r * rows_d + k.start // BLOCK + c] = part[
                        r * BLOCK : (r + 1) * BLOCK, c * BLOCK : (c + 1) * BLOCK
                    ]

    line = sorted(range(1, depth), key=lambda d: (min(d, depth - d), d))
    dist = line[::-1] + [0]
    order = [(ds, df, d) for ds, df in ((1, 1), (1, 0), (0, 1), (0, 0)) for d in dist]
    for i, (ds, df, dz) in enumerate(order):
        chip = at.member(ds, df, dz)
        parts = []
        if not ds:
            parts.append(second_got.at[df * depth + dz])
            got(parts[-1], second_sems.at[df * depth + dz])
        if not ds and not df:
            parts.append(first_got.at[dz])
            got(parts[-1], first_sems.at[dz])
            if not dz:
                for d in range(1, depth):
                    parts.append(line_got.at[d - 1])
                    got(parts[-1], line_sems.at[d - 1])

        def fill(step, carry, i=i, parts=parts, chip=chip):
            half = step // per
            part = pl.ds(pl.multiple_of((step % per) * BLOCK, BLOCK), BLOCK)
            value = grads[pos[chip * (2 * per) + step]]
            if parts:
                value = value.astype(jnp.float32)
                for q in parts:
                    value += q[half, part, :].astype(jnp.float32)
            held[i, half, part, :] = value.astype(jnp.bfloat16)
            return carry

        lax.fori_loop(0, 2 * per, fill, 0)
        if ds:
            start(held.at[i], second_got.at[df * depth + dz], second_sems.at[df * depth + dz], at.device(1, 0, 0))
        elif df:
            start(held.at[i], first_got.at[dz], first_sems.at[dz], at.device(0, 1, 0))
        elif dz:
            start(held.at[i], line_got.at[dz - 1], line_sems.at[dz - 1], at.device(0, 0, dz))
        else:
            last = start(held.at[i, 1 - mine], last_got, pair_sems.at[1], at.sibling)
            out[mine] = held[i, mine]
            last.wait_recv()
    out[1 - mine] = last_got[...]
    for copy in sends:
        copy.wait_send()


def layer_sums(places, begin, tokens, cotangent, other, full, devices, per):
    count, width = tokens.shape
    chips = devices // 2
    depth = devices // 8
    shard = (2, per * BLOCK, BLOCK)
    dma = pltpu.SemaphoreType.DMA
    vmem = pltpu.VMEM
    anywhere = pl.BlockSpec(memory_space=pl.ANY)
    scalars = pl.BlockSpec(memory_space=pltpu.SMEM)
    bf16, f32 = jnp.bfloat16, jnp.float32
    return pl.pallas_call(
        functools.partial(layer_kernel, devices, per),
        out_shape=jax.ShapeDtypeStruct(shard, bf16),
        in_specs=[scalars, scalars, anywhere, anywhere, anywhere, anywhere],
        out_specs=pl.BlockSpec(memory_space=vmem),
        scratch_shapes=[
            vmem((full.shape[0] + 1, BLOCK, BLOCK), bf16),
            vmem((2 * count, width), bf16),
            vmem((width, RANK), bf16),
            vmem((RANK, width), bf16),
            vmem((width * RANK // (BLOCK * BLOCK) + 1, BLOCK, BLOCK), bf16),
            vmem((2 * count, RANK), f32),
            vmem((2 * count, RANK), f32),
            vmem((2 * count, BLOCK), f32),
            vmem((chips,) + shard, bf16),
            vmem((2 * depth,) + shard, bf16),
            vmem((depth,) + shard, bf16),
            vmem((depth - 1,) + shard, bf16),
            vmem(shard[1:], bf16),
            dma((3,)),
            dma((chips + 1,)),
            dma((2 * depth,)),
            dma((depth,)),
            dma((depth - 1,)),
            dma((2,)),
        ],
        compiler_params=pltpu.CompilerParams(
            collective_id=1, has_side_effects=True, vmem_limit_bytes=60 * 1024 * 1024
        ),
        name="layer_sums",
    )(places, begin, tokens, cotangent, other, full)


def one_section(tokens, blocks_in, blocks_out, pos_in, pos_out, cotangent):
    devices = lax.axis_size("dp")
    per = blocks_in.shape[1]
    own = jnp.stack([blocks_in[0], blocks_out[0]])
    places = jnp.concatenate([pos_in, pos_out]).astype(jnp.bfloat16)
    places = jnp.pad(places[:, None, :], ((0, 0), (0, EXTRA - 1), (0, BLOCK - per)))
    full, tags, other = gather_blocks(own, places, tokens, cotangent, devices)
    count = devices * per
    slots = tags[:, 0, :per].astype(jnp.int32)
    starts = per * jnp.arange(devices)[:, None] + jnp.arange(per)[None, :]
    numbers = jnp.arange((tokens.shape[1] // BLOCK) * (RANK // BLOCK))
    found = jnp.where(slots[None] == numbers[:, None, None], starts[None], count)
    begin = jnp.min(found, axis=(1, 2)).astype(jnp.int32)
    flat = full.reshape(count, BLOCK, BLOCK)
    sums = layer_sums(slots.reshape(-1), begin, tokens, cotangent, other, flat, devices, per)
    shape = blocks_in.shape
    return (sums[0].reshape(shape), sums[1].reshape(shape))


def solution(mesh):
    in_specs = (
        P("dp", None),
        P("section", "dp", None, None),
        P("section", "dp", None, None),
        P("section", "dp"),
        P("section", "dp"),
        P("dp", None),
    )
    out_specs = (P("section", "dp", None, None), P("section", "dp", None, None))
    body = one_section if mesh.shape["section"] == 1 else per_device
    return jax.shard_map(
        body, mesh=mesh, in_specs=in_specs, out_specs=out_specs, check_vma=False
    )
```

```python
import functools

import jax
import jax.numpy as jnp
from jax import lax
from jax.experimental import pallas as pl
from jax.experimental.pallas import tpu as pltpu
from jax.sharding import PartitionSpec as P

D = 8192
RANK = 512
BLOCK = 128
MICRO = 2


EPS = 1e-05


def from_behind(block, axis, distance):
    devices = range(lax.axis_size(axis))
    route = [(i - distance, i) for i in devices if i - distance in devices]
    return lax.ppermute(block, axis, route)


def expand(blocks, places, rows_b, cols_b):
    flat = jnp.zeros((rows_b * cols_b, BLOCK, BLOCK), blocks.dtype)
    flat = flat.at[places].set(blocks, mode="drop")
    return (
        flat.reshape(rows_b, cols_b, BLOCK, BLOCK)
        .transpose(0, 2, 1, 3)
        .reshape(rows_b * BLOCK, cols_b * BLOCK)
    )


def slot_grads(left, right, places, rows_b, cols_b):
    count = left.shape[0]
    valid = places < rows_b * cols_b
    row_block = jnp.where(valid, places // cols_b, 0).astype(jnp.int32)
    col_block = jnp.where(valid, places % cols_b, 0).astype(jnp.int32)
    left_blocks = jnp.take(left.reshape(count, rows_b, BLOCK), row_block, axis=1)
    right_blocks = jnp.take(right.reshape(count, cols_b, BLOCK), col_block, axis=1)
    result = jnp.einsum(
        "tjb,tjc->jbc", left_blocks, right_blocks, preferred_element_type=jnp.float32
    )
    return jnp.where(valid[:, None, None], result, 0.0)


def norm_parts(hidden):
    wide = hidden.astype(jnp.float32)
    scale = jnp.sqrt(jnp.mean(wide * wide, axis=-1, keepdims=True) + EPS)
    return (wide, scale)


def forward_layer(hidden, mat_a, mat_b):
    wide, scale = norm_parts(hidden)
    normed = (wide / scale).astype(jnp.bfloat16)
    pre = jnp.dot(normed, mat_a, preferred_element_type=jnp.float32)
    act = (pre * jax.nn.sigmoid(pre)).astype(jnp.bfloat16)
    return (wide + jnp.dot(act, mat_b, preferred_element_type=jnp.float32)).astype(jnp.bfloat16)


def backward_layer(hidden, upstream, mat_a, mat_b):
    wide, scale = norm_parts(hidden)
    unit = wide / scale
    normed = unit.astype(jnp.bfloat16)
    pre = jnp.dot(normed, mat_a, preferred_element_type=jnp.float32)
    sig = jax.nn.sigmoid(pre)
    act = (pre * sig).astype(jnp.bfloat16)
    dact = lax.dot_general(
        upstream, mat_b, (((1,), (1,)), ((), ())), preferred_element_type=jnp.float32
    )
    dpre = (dact * sig * (1.0 + pre * (1.0 - sig))).astype(jnp.bfloat16)
    dnorm = lax.dot_general(
        dpre, mat_a, (((1,), (1,)), ((), ())), preferred_element_type=jnp.float32
    )
    inner = jnp.mean(dnorm * unit, axis=-1, keepdims=True)
    earlier = (upstream.astype(jnp.float32) + (dnorm - unit * inner) / scale).astype(jnp.bfloat16)
    return (earlier, normed, dpre, act)


def store(stack, value, picked, active):
    updated = lax.dynamic_update_slice_in_dim(stack, value[None], picked, 0)
    return jnp.where(active, updated, stack)


def per_device(tokens, blocks_in, blocks_out, pos_in, pos_out, cotangent):
    sections = lax.axis_size("section")
    here = lax.axis_index("section")
    rows_d = D // BLOCK
    rows_k = RANK // BLOCK
    full_in, full_out, all_in, all_out = (
        lax.all_gather(blocks_in, "dp", axis=1, tiled=True),
        lax.all_gather(blocks_out, "dp", axis=1, tiled=True),
        lax.all_gather(pos_in, "dp", axis=1, tiled=True),
        lax.all_gather(pos_out, "dp", axis=1, tiled=True),
    )
    mat_a = expand(full_in[0], all_in[0], rows_d, rows_k)
    mat_b = expand(full_out[0], all_out[0], rows_k, rows_d)
    micro_rows = tokens.shape[0] // MICRO
    turns = MICRO + sections - 1
    saved = jnp.zeros((MICRO, micro_rows, D), jnp.bfloat16)
    carried = jnp.zeros((micro_rows, D), jnp.bfloat16)
    for turn in range(turns):
        micro = turn - here
        active = (micro >= 0) & (micro < MICRO)
        picked = jnp.clip(micro, 0, MICRO - 1)
        first = lax.dynamic_slice_in_dim(tokens, picked * micro_rows, micro_rows, 0)
        entering = jnp.where(here == 0, first, carried)
        saved = store(saved, entering, picked, active)
        if turn < turns - 1:
            leaving = lax.cond(
                active, lambda x: forward_layer(x, mat_a, mat_b), lambda x: x, entering
            )
            carried = from_behind(leaving, "section", 1)
    kept_normed = jnp.zeros((MICRO, micro_rows, D), jnp.bfloat16)
    kept_dpre = jnp.zeros((MICRO, micro_rows, RANK), jnp.bfloat16)
    kept_act = jnp.zeros((MICRO, micro_rows, RANK), jnp.bfloat16)
    kept_upper = jnp.zeros((MICRO, micro_rows, D), jnp.bfloat16)
    carried_grad = jnp.zeros((micro_rows, D), jnp.bfloat16)
    for turn in range(turns):
        micro = turn - (sections - 1 - here)
        active = (micro >= 0) & (micro < MICRO)
        picked = jnp.clip(micro, 0, MICRO - 1)
        last = lax.dynamic_slice_in_dim(cotangent, picked * micro_rows, micro_rows, 0)
        upstream = jnp.where(here == sections - 1, last, carried_grad)
        hidden = lax.dynamic_index_in_dim(saved, picked, 0, keepdims=False)

        def run_layer():
            return backward_layer(hidden, upstream, mat_a, mat_b)

        def skip_layer():
            return (
                upstream,
                jnp.zeros((micro_rows, D), jnp.bfloat16),
                jnp.zeros((micro_rows, RANK), jnp.bfloat16),
                jnp.zeros((micro_rows, RANK), jnp.bfloat16),
            )

        earlier, normed, dpre, act = lax.cond(active, run_layer, skip_layer)
        kept_normed = store(kept_normed, normed, picked, active)
        kept_dpre = store(kept_dpre, dpre, picked, active)
        kept_act = store(kept_act, act, picked, active)
        kept_upper = store(kept_upper, upstream, picked, active)
        if turn < turns - 1:
            carried_grad = from_behind(earlier, "section", -1)
    all_rows = MICRO * micro_rows
    terms_in = slot_grads(
        kept_normed.reshape(all_rows, D),
        kept_dpre.reshape(all_rows, RANK),
        all_in[0],
        rows_d,
        rows_k,
    )[None]
    terms_out = slot_grads(
        kept_act.reshape(all_rows, RANK),
        kept_upper.reshape(all_rows, D),
        all_out[0],
        rows_k,
        rows_d,
    )[None]
    sums_in, sums_out = (
        lax.psum_scatter(
            terms_in.astype(jnp.bfloat16), "dp", scatter_dimension=1, tiled=True
        ).astype(jnp.float32),
        lax.psum_scatter(
            terms_out.astype(jnp.bfloat16), "dp", scatter_dimension=1, tiled=True
        ).astype(jnp.float32),
    )
    return (sums_in.astype(jnp.bfloat16), sums_out.astype(jnp.bfloat16))


EXTRA= 16
WIDE = 1024


class Place:
    def __init__(self, devices):
        me = lax.axis_index("dp")
        self.depth = devices // 8
        self.me = me
        self.core = me % 2
        self.chip = me // 2
        x = self.chip % 2
        y = (self.chip // 2) % 2
        self.z = self.chip // 4
        dx = 1 - 2 * x
        dy = 2 * (1 - 2 * y)
        self.first = (1 - self.core) * dx + self.core * dy
        self.second = (1 - self.core) * dy + self.core * dx
        self.sibling = me + 1 - 2 * self.core

    def member(self, ds, df, dz, first=None, second=None):
        first = self.first if first is None else first
        second = self.second if second is None else second
        along = ((self.z + dz) % self.depth - self.z) * 4
        return self.chip + along + df * first + ds * second

    def device(self, ds, df, dz):
        return 2 * self.member(ds, df, dz) + self.core

    def knock(self):
        peers = [self.sibling, self.device(1, 0, 0), self.device(0, 1, 0)]
        peers += [self.device(0, 0, d) for d in range(1, self.depth)]
        barrier = pltpu.get_barrier_semaphore()
        for peer in peers:
            pl.semaphore_signal(
                barrier, inc=1, device_id={"dp": peer}, device_id_type=pl.DeviceIdType.MESH
            )
        return lambda: pl.semaphore_wait(barrier, len(peers))


def remote(src, dst, send, recv, peer):
    return pltpu.make_async_remote_copy(
        src_ref=src,
        dst_ref=dst,
        send_sem=send,
        recv_sem=recv,
        device_id={"dp": peer},
        device_id_type=pl.DeviceIdType.MESH,
    )


def gather_kernel(
    devices, own_in, own_out, own_tags, tokens, cotangent, full, tags, other, send_sems, chip_sems, misc_sems
):
    at = Place(devices)
    depth = at.depth
    mine = at.core
    sends = []

    def on_core(core):
        return pl.when(mine == core)

    def local_copy(source):
        return pltpu.make_async_copy(source, full.at[at.me], misc_sems.at[0])

    on_core(0)(lambda: local_copy(own_in).start())
    on_core(1)(lambda: local_copy(own_out).start())
    local = [
        local_copy(own_in),
        pltpu.make_async_copy(own_tags.at[mine], tags.at[at.me], misc_sems.at[3]),
    ]
    local[1].start()
    at.knock()()

    def start(src, dst, recv, peer, like, present=None):
        remote(src, dst, send_sems.at[len(sends)], recv, peer).start()
        sends.append((like, present))

    def pair_copy(source):
        return remote(source, full.at[at.me], send_sems.at[0], misc_sems.at[1], at.sibling)

    on_core(0)(lambda: pair_copy(own_out).start())
    on_core(1)(lambda: pair_copy(own_in).start())
    sends.append((own_in, None))
    start(own_tags.at[1 - mine], tags.at[at.me], misc_sems.at[4], at.sibling, own_tags.at[0])
    pair = [
        pair_copy(own_in),
        remote(own_tags.at[0], tags.at[at.me], send_sems.at[0], misc_sems.at[4], at.sibling),
    ]

    def shards(chip):
        return (
            (full.at[pl.ds(2 * chip, 2)], chip_sems.at[0, chip]),
            (tags.at[pl.ds(2 * chip, 2)], chip_sems.at[1, chip]),
        )

    def push(chip, peer, present=None):
        for (shard, sem), like in zip(shards(chip), (full.at[pl.ds(0, 2)], tags.at[pl.ds(0, 2)])):
            start(shard, shard, sem, peer, like, present)

    def arrived(chip):
        for shard, sem in shards(chip):
            remote(shard, shard, send_sems.at[0], sem, at.sibling).wait_recv()

    first, second = at.device(0, 1, 0), at.device(1, 0, 0)
    above, below = at.me + 8, at.me - 8
    up, down = at.z + 1 < depth, at.z >= 1
    for copy in local:
        copy.wait()
    for copy in pair:
        copy.wait_recv()
    here = at.chip
    pl.when(up)(lambda: push(here, above, lambda: up))
    pl.when(down)(lambda: push(here, below, lambda: down))
    push(here, second)
    push(here, first)
    swap = misc_sems.at[2]
    give = remote(tokens, other, send_sems.at[len(sends)], swap, at.sibling)
    keep = remote(cotangent, other, send_sems.at[len(sends)], swap, at.sibling)
    on_core(0)(lambda: keep.start())
    on_core(1)(lambda: give.start())
    sends.append((tokens, None))
    facing = here + at.first
    arrived(facing)
    push(facing, second)
    for d in range(1, depth):
        low, high = at.z >= d, at.z + d < depth

        def from_below(d=d, low=low):
            arrived(here - 4 * d)
            pl.when(up)(lambda: push(here - 4 * d, above, lambda: low & up))
            push(here - 4 * d, first, lambda: low)
            push(here - 4 * d, second, lambda: low)

        def from_above(d=d, high=high):
            arrived(here + 4 * d)
            pl.when(down)(lambda: push(here + 4 * d, below, lambda: high & down))
            push(here + 4 * d, first, lambda: high)
            push(here + 4 * d, second, lambda: high)

        def relay_below(d=d, low=low):
            arrived(facing - 4 * d)
            push(facing - 4 * d, second, lambda: low)

        def relay_above(d=d, high=high):
            arrived(facing + 4 * d)
            push(facing + 4 * d, second, lambda: high)

        pl.when(low)(from_below)
        pl.when(high)(from_above)
        pl.when(low)(relay_below)
        pl.when(high)(relay_above)
    for df in range(2):
        for d in range(depth):
            arrived(at.member(1, df, d))
    give.wait_recv()
    for n, (like, present) in enumerate(sends):

        def sent(n=n, like=like):
            remote(like, like, send_sems.at[n], misc_sems.at[0], at.sibling).wait_send()

        if present is None:
            sent()
        else:
            pl.when(present())(sent)


def gather_blocks(own_in, own_out, own_tags, tokens, cotangent, devices):
    chips = devices // 2
    depth = devices // 8
    sends = 2 * (1 + 2 + 2 + 1 + 8 * (depth - 1)) + 1
    anywhere = pl.BlockSpec(memory_space=pl.ANY)
    return pl.pallas_call(
        functools.partial(gather_kernel, devices),
        out_shape=(
            jax.ShapeDtypeStruct((devices,) + own_in.shape, own_in.dtype),
            jax.ShapeDtypeStruct((devices,) + own_tags.shape[1:], own_tags.dtype),
            jax.ShapeDtypeStruct(tokens.shape, tokens.dtype),
        ),
        in_specs=[pl.BlockSpec(memory_space=pltpu.VMEM)] * 3 + [anywhere, anywhere],
        out_specs=(anywhere, anywhere, anywhere),
        scratch_shapes=[
            pltpu.SemaphoreType.DMA((sends,)),
            pltpu.SemaphoreType.DMA((2, chips)),
            pltpu.SemaphoreType.DMA((5,)),
        ],
        compiler_params=pltpu.CompilerParams(collective_id=0, has_side_effects=True),
        name="gather_blocks",
    )(own_in, own_out, own_tags, tokens, cotangent)


def layer_kernel(devices, per, pos, begin, tokens, cotangent, other, full, out,
                 blocks, rows, mat_a, mat_b, grads, middle, middle_got, inverse,
                 held, second_got, first_got, line_got, last_got,
                 load_sems, send_sems, second_sems, first_sems, line_sems, pair_sems):
    at = Place(devices)
    depth = at.depth
    mine = at.core
    count, width = tokens.shape
    rank = mat_a.shape[1]
    rows_k = rank // BLOCK
    rows_d = width // BLOCK
    chunks = [slice(i, i + WIDE) for i in range(0, width, WIDE)]
    sends = []

    def start(src, dst, recv, peer):
        copy = remote(src, dst, send_sems.at[len(sends)], recv, peer)
        copy.start()
        sends.append(copy)
        return copy

    def got(buf, sem):
        remote(buf, buf, send_sems.at[0], sem, at.sibling).wait_recv()

    used = full.shape[0]
    load_blocks = pltpu.make_async_copy(full, blocks.at[pl.ds(0, used)], load_sems.at[0])
    load_blocks.start()
    load_own = pltpu.make_async_copy(tokens, rows.at[pl.ds(mine * count, count)], load_sems.at[1])

    @pl.when(mine == 0)
    def _():
        load_own.start()

    @pl.when(mine == 1)
    def _():
        pltpu.make_async_copy(cotangent, rows.at[pl.ds(mine * count, count)], load_sems.at[1]).start()

    load_other = pltpu.make_async_copy(other, rows.at[pl.ds((1 - mine) * count, count)], load_sems.at[2])
    load_other.start()
    wait_peers = at.knock()
    blocks[used] = jnp.zeros((BLOCK, BLOCK), jnp.bfloat16)
    grads[rows_d * rows_k] = jnp.zeros((BLOCK, BLOCK), jnp.bfloat16)
    load_blocks.wait()

    def slot_of(b):
        return blocks[begin[b]]

    @pl.when(mine == 0)
    def _():
        def expand_a(r, carry):
            into = pl.ds(pl.multiple_of(r * BLOCK, BLOCK), BLOCK)
            for c in range(rows_k):
                mat_a[into, c * BLOCK : (c + 1) * BLOCK] = slot_of(r * rows_k + c)
            return carry

        lax.fori_loop(0, rows_d, expand_a, 0)

    @pl.when(mine == 1)
    def _():
        def expand_b(c, carry):
            into = pl.ds(pl.multiple_of(c * BLOCK, BLOCK), BLOCK)
            for r in range(rows_k):
                mat_b[r * BLOCK : (r + 1) * BLOCK, into] = slot_of(r * rows_d + c)
            return carry

        lax.fori_loop(0, rows_d, expand_b, 0)

    load_own.wait()
    load_other.wait()

    @pl.when(mine == 0)
    def _():
        total = jnp.zeros((2 * count, BLOCK), jnp.float32)
        for k in range(0, width, BLOCK):
            wide = rows[:, k : k + BLOCK].astype(jnp.float32)
            total += wide * wide
        scale = jnp.sqrt(jnp.sum(total, axis=-1, keepdims=True) / width + EPS)
        inverse[...] = jnp.broadcast_to(1.0 / scale, inverse.shape)
        pre = jnp.zeros((2 * count, rank), jnp.float32)
        for k in chunks:
            pre += jnp.dot(rows[:, k], mat_a[k, :], preferred_element_type=jnp.float32)
        middle[...] = pre * inverse[:, :1]

    @pl.when(mine == 1)
    def _():
        dact = jnp.zeros((2 * count, rank), jnp.float32)
        for k in chunks:
            dact += lax.dot_general(
                rows[:, k], mat_b[:, k], (((1,), (1,)), ((), ())), preferred_element_type=jnp.float32
            )
        middle[...] = dact

    wait_peers()
    start(middle, middle_got, pair_sems.at[0], at.sibling).wait_recv()
    across = (((0,), (0,)), ((), ()))

    @pl.when(mine == 0)
    def _():
        pre = middle[...]
        sig = jax.nn.sigmoid(pre)
        dpre = middle_got[...] * sig * (1.0 + pre * (1.0 - sig))
        dpre = (dpre * inverse[:, :1]).astype(jnp.bfloat16)
        for k in chunks:
            part = lax.dot_general(
                rows[:, k], dpre, across, preferred_element_type=jnp.float32
            ).astype(jnp.bfloat16)
            for r in range(WIDE // BLOCK):
                for c in range(rows_k):
                    grads[(k.start // BLOCK + r) * rows_k + c] = part[
                        r * BLOCK : (r + 1) * BLOCK, c * BLOCK : (c + 1) * BLOCK
                    ]

    @pl.when(mine == 1)
    def _():
        pre = middle_got[...]
        act = (pre * jax.nn.sigmoid(pre)).astype(jnp.bfloat16)
        for k in chunks:
            part = lax.dot_general(
                act, rows[:, k], across, preferred_element_type=jnp.float32
            ).astype(jnp.bfloat16)
            for r in range(rows_k):
                for c in range(WIDE // BLOCK):
                    grads[r * rows_d + k.start // BLOCK + c] = part[
                        r * BLOCK : (r + 1) * BLOCK, c * BLOCK : (c + 1) * BLOCK
                    ]

    line = sorted(range(1, depth), key=lambda d: (min(d, depth - d), d))
    dist = line[::-1] + [0]
    order = [(ds, df, d) for ds in (1, 0) for d in dist for df in (1, 0)]
    for i, (ds, df, dz) in enumerate(order):
        chip = at.member(ds, df, dz)
        parts = []
        if not ds:
            parts.append(second_got.at[df * depth + dz])
            got(parts[-1], second_sems.at[df * depth + dz])
        if not ds and not df:
            parts.append(first_got.at[dz])
            got(parts[-1], first_sems.at[dz])
            if not dz:
                for d in range(1, depth):
                    parts.append(line_got.at[d - 1])
                    got(parts[-1], line_sems.at[d - 1])

        def fill(step, carry, i=i, parts=parts, chip=chip):
            half = step // per
            part = pl.ds(pl.multiple_of((step % per) * BLOCK, BLOCK), BLOCK)
            value = grads[pos[chip * (2 * per) + step]]
            if parts:
                value = value.astype(jnp.float32)
                for q in parts:
                    value += q[half, part, :].astype(jnp.float32)
            held[i, half, part, :] = value.astype(jnp.bfloat16)
            return carry

        lax.fori_loop(0, 2 * per, fill, 0)
        if ds:
            start(held.at[i], second_got.at[df * depth + dz], second_sems.at[df * depth + dz], at.device(1, 0, 0))
        elif df:
            start(held.at[i], first_got.at[dz], first_sems.at[dz], at.device(0, 1, 0))
        elif dz:
            start(held.at[i], line_got.at[dz - 1], line_sems.at[dz - 1], at.device(0, 0, dz))
        else:
            last = start(held.at[i, 1 - mine], last_got, pair_sems.at[1], at.sibling)
            out[mine] = held[i, mine]
            last.wait_recv()
    out[1 - mine] = last_got[...]
    for copy in sends:
        copy.wait_send()


def layer_sums(places, begin, tokens, cotangent, other, full, devices, per):
    count, width = tokens.shape
    chips = devices // 2
    depth = devices // 8
    shard = (2, per * BLOCK, BLOCK)
    dma = pltpu.SemaphoreType.DMA
    vmem = pltpu.VMEM
    anywhere = pl.BlockSpec(memory_space=pl.ANY)
    scalars = pl.BlockSpec(memory_space=pltpu.SMEM)
    bf16, f32 = jnp.bfloat16, jnp.float32
    return pl.pallas_call(
        functools.partial(layer_kernel, devices, per),
        out_shape=jax.ShapeDtypeStruct(shard, bf16),
        in_specs=[scalars, scalars, anywhere, anywhere, anywhere, anywhere],
        out_specs=pl.BlockSpec(memory_space=vmem),
        scratch_shapes=[
            vmem((full.shape[0] + 1, BLOCK, BLOCK), bf16),
            vmem((2 * count, width), bf16),
            vmem((width, RANK), bf16),
            vmem((RANK, width), bf16),
            vmem((width * RANK // (BLOCK * BLOCK) + 1, BLOCK, BLOCK), bf16),
            vmem((2 * count, RANK), f32),
            vmem((2 * count, RANK), f32),
            vmem((2 * count, BLOCK), f32),
            vmem((chips,) + shard, bf16),
            vmem((2 * depth,) + shard, bf16),
            vmem((depth,) + shard, bf16),
            vmem((depth - 1,) + shard, bf16),
            vmem(shard[1:], bf16),
            dma((3,)),
            dma((chips + 1,)),
            dma((2 * depth,)),
            dma((depth,)),
            dma((depth - 1,)),
            dma((2,)),
        ],
        compiler_params=pltpu.CompilerParams(
            collective_id=1, has_side_effects=True, vmem_limit_bytes=60 * 1024 * 1024
        ),
        name="layer_sums",
    )(places, begin, tokens, cotangent, other, full)


def one_section(tokens, blocks_in, blocks_out, pos_in, pos_out, cotangent):
    devices = lax.axis_size("dp")
    per = blocks_in.shape[1]
    places = jnp.concatenate([pos_in, pos_out]).astype(jnp.bfloat16)
    places = jnp.pad(places[:, None, :], ((0, 0), (0, EXTRA - 1), (0, BLOCK - per)))
    full, tags, other = gather_blocks(blocks_in[0], blocks_out[0], places, tokens, cotangent, devices)
    count = devices * per
    slots = tags[:, 0, :per].astype(jnp.int32)
    starts = per * jnp.arange(devices)[:, None] + jnp.arange(per)[None, :]
    numbers = jnp.arange((tokens.shape[1] // BLOCK) * (RANK // BLOCK))
    found = jnp.where(slots[None] == numbers[:, None, None], starts[None], count)
    begin = jnp.min(found, axis=(1, 2)).astype(jnp.int32)
    flat = full.reshape(count, BLOCK, BLOCK)
    sums = layer_sums(slots.reshape(-1), begin, tokens, cotangent, other, flat, devices, per)
    shape = blocks_in.shape
    return (sums[0].reshape(shape), sums[1].reshape(shape))


def solution(mesh):
    in_specs = (
        P("dp", None),
        P("section", "dp", None, None),
        P("section", "dp", None, None),
        P("section", "dp"),
        P("section", "dp"),
        P("dp", None),
    )
    out_specs = (P("section", "dp", None, None), P("section", "dp", None, None))
    body = one_section if mesh.shape["section"] == 1 else per_device
    return jax.shard_map(
        body, mesh=mesh, in_specs=in_specs, out_specs=out_specs, check_vma=False
    )
```

```python
import functools

import jax
import jax.numpy as jnp
from jax import lax
from jax.experimental import pallas as pl
from jax.experimental.pallas import tpu as pltpu
from jax.sharding import PartitionSpec as P

D = 8192
RANK = 512
BLOCK = 128
MICRO = 2


EPS = 1e-05


def from_behind(block, axis, distance):
    devices = range(lax.axis_size(axis))
    route = [(i - distance, i) for i in devices if i - distance in devices]
    return lax.ppermute(block, axis, route)


def expand(blocks, places, rows_b, cols_b):
    flat = jnp.zeros((rows_b * cols_b, BLOCK, BLOCK), blocks.dtype)
    flat = flat.at[places].set(blocks, mode="drop")
    return (
        flat.reshape(rows_b, cols_b, BLOCK, BLOCK)
        .transpose(0, 2, 1, 3)
        .reshape(rows_b * BLOCK, cols_b * BLOCK)
    )


def slot_grads(left, right, places, rows_b, cols_b):
    count = left.shape[0]
    valid = places < rows_b * cols_b
    row_block = jnp.where(valid, places // cols_b, 0).astype(jnp.int32)
    col_block = jnp.where(valid, places % cols_b, 0).astype(jnp.int32)
    left_blocks = jnp.take(left.reshape(count, rows_b, BLOCK), row_block, axis=1)
    right_blocks = jnp.take(right.reshape(count, cols_b, BLOCK), col_block, axis=1)
    result = jnp.einsum(
        "tjb,tjc->jbc", left_blocks, right_blocks, preferred_element_type=jnp.float32
    )
    return jnp.where(valid[:, None, None], result, 0.0)


def norm_parts(hidden):
    wide = hidden.astype(jnp.float32)
    scale = jnp.sqrt(jnp.mean(wide * wide, axis=-1, keepdims=True) + EPS)
    return (wide, scale)


def forward_layer(hidden, mat_a, mat_b):
    wide, scale = norm_parts(hidden)
    normed = (wide / scale).astype(jnp.bfloat16)
    pre = jnp.dot(normed, mat_a, preferred_element_type=jnp.float32)
    act = (pre * jax.nn.sigmoid(pre)).astype(jnp.bfloat16)
    return (wide + jnp.dot(act, mat_b, preferred_element_type=jnp.float32)).astype(jnp.bfloat16)


def backward_layer(hidden, upstream, mat_a, mat_b):
    wide, scale = norm_parts(hidden)
    unit = wide / scale
    normed = unit.astype(jnp.bfloat16)
    pre = jnp.dot(normed, mat_a, preferred_element_type=jnp.float32)
    sig = jax.nn.sigmoid(pre)
    act = (pre * sig).astype(jnp.bfloat16)
    dact = lax.dot_general(
        upstream, mat_b, (((1,), (1,)), ((), ())), preferred_element_type=jnp.float32
    )
    dpre = (dact * sig * (1.0 + pre * (1.0 - sig))).astype(jnp.bfloat16)
    dnorm = lax.dot_general(
        dpre, mat_a, (((1,), (1,)), ((), ())), preferred_element_type=jnp.float32
    )
    inner = jnp.mean(dnorm * unit, axis=-1, keepdims=True)
    earlier = (upstream.astype(jnp.float32) + (dnorm - unit * inner) / scale).astype(jnp.bfloat16)
    return (earlier, normed, dpre, act)


def store(stack, value, picked, active):
    updated = lax.dynamic_update_slice_in_dim(stack, value[None], picked, 0)
    return jnp.where(active, updated, stack)


def per_device(tokens, blocks_in, blocks_out, pos_in, pos_out, cotangent):
    sections = lax.axis_size("section")
    here = lax.axis_index("section")
    rows_d = D // BLOCK
    rows_k = RANK // BLOCK
    full_in, full_out, all_in, all_out = (
        lax.all_gather(blocks_in, "dp", axis=1, tiled=True),
        lax.all_gather(blocks_out, "dp", axis=1, tiled=True),
        lax.all_gather(pos_in, "dp", axis=1, tiled=True),
        lax.all_gather(pos_out, "dp", axis=1, tiled=True),
    )
    mat_a = expand(full_in[0], all_in[0], rows_d, rows_k)
    mat_b = expand(full_out[0], all_out[0], rows_k, rows_d)
    micro_rows = tokens.shape[0] // MICRO
    turns = MICRO + sections - 1
    saved = jnp.zeros((MICRO, micro_rows, D), jnp.bfloat16)
    carried = jnp.zeros((micro_rows, D), jnp.bfloat16)
    for turn in range(turns):
        micro = turn - here
        active = (micro >= 0) & (micro < MICRO)
        picked = jnp.clip(micro, 0, MICRO - 1)
        first = lax.dynamic_slice_in_dim(tokens, picked * micro_rows, micro_rows, 0)
        entering = jnp.where(here == 0, first, carried)
        saved = store(saved, entering, picked, active)
        if turn < turns - 1:
            leaving = lax.cond(
                active, lambda x: forward_layer(x, mat_a, mat_b), lambda x: x, entering
            )
            carried = from_behind(leaving, "section", 1)
    kept_normed = jnp.zeros((MICRO, micro_rows, D), jnp.bfloat16)
    kept_dpre = jnp.zeros((MICRO, micro_rows, RANK), jnp.bfloat16)
    kept_act = jnp.zeros((MICRO, micro_rows, RANK), jnp.bfloat16)
    kept_upper = jnp.zeros((MICRO, micro_rows, D), jnp.bfloat16)
    carried_grad = jnp.zeros((micro_rows, D), jnp.bfloat16)
    for turn in range(turns):
        micro = turn - (sections - 1 - here)
        active = (micro >= 0) & (micro < MICRO)
        picked = jnp.clip(micro, 0, MICRO - 1)
        last = lax.dynamic_slice_in_dim(cotangent, picked * micro_rows, micro_rows, 0)
        upstream = jnp.where(here == sections - 1, last, carried_grad)
        hidden = lax.dynamic_index_in_dim(saved, picked, 0, keepdims=False)

        def run_layer():
            return backward_layer(hidden, upstream, mat_a, mat_b)

        def skip_layer():
            return (
                upstream,
                jnp.zeros((micro_rows, D), jnp.bfloat16),
                jnp.zeros((micro_rows, RANK), jnp.bfloat16),
                jnp.zeros((micro_rows, RANK), jnp.bfloat16),
            )

        earlier, normed, dpre, act = lax.cond(active, run_layer, skip_layer)
        kept_normed = store(kept_normed, normed, picked, active)
        kept_dpre = store(kept_dpre, dpre, picked, active)
        kept_act = store(kept_act, act, picked, active)
        kept_upper = store(kept_upper, upstream, picked, active)
        if turn < turns - 1:
            carried_grad = from_behind(earlier, "section", -1)
    all_rows = MICRO * micro_rows
    terms_in = slot_grads(
        kept_normed.reshape(all_rows, D),
        kept_dpre.reshape(all_rows, RANK),
        all_in[0],
        rows_d,
        rows_k,
    )[None]
    terms_out = slot_grads(
        kept_act.reshape(all_rows, RANK),
        kept_upper.reshape(all_rows, D),
        all_out[0],
        rows_k,
        rows_d,
    )[None]
    sums_in, sums_out = (
        lax.psum_scatter(
            terms_in.astype(jnp.bfloat16), "dp", scatter_dimension=1, tiled=True
        ).astype(jnp.float32),
        lax.psum_scatter(
            terms_out.astype(jnp.bfloat16), "dp", scatter_dimension=1, tiled=True
        ).astype(jnp.float32),
    )
    return (sums_in.astype(jnp.bfloat16), sums_out.astype(jnp.bfloat16))


EXTRA= 16
WIDE = 1024


class Place:
    def __init__(self, devices):
        me = lax.axis_index("dp")
        self.depth = devices // 8
        self.me = me
        self.core = me % 2
        self.chip = me // 2
        x = self.chip % 2
        y = (self.chip // 2) % 2
        self.z = self.chip // 4
        dx = 1 - 2 * x
        dy = 2 * (1 - 2 * y)
        self.first = (1 - self.core) * dx + self.core * dy
        self.second = (1 - self.core) * dy + self.core * dx
        self.sibling = me + 1 - 2 * self.core

    def member(self, ds, df, dz, first=None, second=None):
        first = self.first if first is None else first
        second = self.second if second is None else second
        along = ((self.z + dz) % self.depth - self.z) * 4
        return self.chip + along + df * first + ds * second

    def device(self, ds, df, dz):
        return 2 * self.member(ds, df, dz) + self.core

    def knock(self):
        peers = [self.sibling, self.device(1, 0, 0), self.device(0, 1, 0)]
        peers += [self.device(0, 0, d) for d in range(1, self.depth)]
        barrier = pltpu.get_barrier_semaphore()
        for peer in peers:
            pl.semaphore_signal(
                barrier, inc=1, device_id={"dp": peer}, device_id_type=pl.DeviceIdType.MESH
            )
        return lambda: pl.semaphore_wait(barrier, len(peers))


def remote(src, dst, send, recv, peer):
    return pltpu.make_async_remote_copy(
        src_ref=src,
        dst_ref=dst,
        send_sem=send,
        recv_sem=recv,
        device_id={"dp": peer},
        device_id_type=pl.DeviceIdType.MESH,
    )


def gather_kernel(
    devices, own_in, own_out, own_tags, tokens, cotangent, full, tags, other, send_sems, chip_sems, misc_sems
):
    at = Place(devices)
    depth = at.depth
    mine = at.core
    sends = []

    def on_core(core):
        return pl.when(mine == core)

    def local_copy(source):
        return pltpu.make_async_copy(source, full.at[at.me], misc_sems.at[0])

    on_core(0)(lambda: local_copy(own_in).start())
    on_core(1)(lambda: local_copy(own_out).start())
    local = [
        local_copy(own_in),
        pltpu.make_async_copy(own_tags.at[mine], tags.at[at.me], misc_sems.at[3]),
    ]
    local[1].start()
    at.knock()()

    def start(src, dst, recv, peer, like, present=None):
        remote(src, dst, send_sems.at[len(sends)], recv, peer).start()
        sends.append((like, present))

    def pair_copy(source):
        return remote(source, full.at[at.me], send_sems.at[0], misc_sems.at[1], at.sibling)

    on_core(0)(lambda: pair_copy(own_out).start())
    on_core(1)(lambda: pair_copy(own_in).start())
    sends.append((own_in, None))
    start(own_tags.at[1 - mine], tags.at[at.me], misc_sems.at[4], at.sibling, own_tags.at[0])
    pair = [
        pair_copy(own_in),
        remote(own_tags.at[0], tags.at[at.me], send_sems.at[0], misc_sems.at[4], at.sibling),
    ]

    per = own_in.shape[0]
    bulk = full.at[pl.ds(0, 2), pl.ds(0, per - 1)]
    spare = full.at[pl.ds(0, 2), pl.ds(per - 1, 1)]

    def odd(chip):
        return full.at[pl.ds(2 * chip, 2), pl.ds(per - 1, 1)]

    def push_odd(chip, peer, present=None):
        start(odd(chip), odd(chip), chip_sems.at[2, chip], peer, spare, present)

    def odd_arrived(chip):
        remote(odd(chip), odd(chip), send_sems.at[0], chip_sems.at[2, chip], at.sibling).wait_recv()

    def shards(chip):
        return (
            (full.at[pl.ds(2 * chip, 2), pl.ds(0, per - 1)], chip_sems.at[0, chip]),
            (tags.at[pl.ds(2 * chip, 2)], chip_sems.at[1, chip]),
        )

    def push(chip, peer, present=None):
        for (shard, sem), like in zip(shards(chip), (bulk, tags.at[pl.ds(0, 2)])):
            start(shard, shard, sem, peer, like, present)

    def arrived(chip):
        for shard, sem in shards(chip):
            remote(shard, shard, send_sems.at[0], sem, at.sibling).wait_recv()

    first, second = at.device(0, 1, 0), at.device(1, 0, 0)
    above, below = at.me + 8, at.me - 8
    up, down = at.z + 1 < depth, at.z >= 1
    for copy in local:
        copy.wait()
    for copy in pair:
        copy.wait_recv()
    here = at.chip
    pl.when(up)(lambda: push(here, above, lambda: up))
    pl.when(down)(lambda: push(here, below, lambda: down))
    push(here, second)
    push(here, first)
    push_odd(here, first)
    push_odd(here, second)
    pl.when(up)(lambda: push_odd(here, above, lambda: up))
    pl.when(down)(lambda: push_odd(here, below, lambda: down))
    swap = misc_sems.at[2]
    give = remote(tokens, other, send_sems.at[len(sends)], swap, at.sibling)
    keep = remote(cotangent, other, send_sems.at[len(sends)], swap, at.sibling)
    on_core(0)(lambda: keep.start())
    on_core(1)(lambda: give.start())
    sends.append((tokens, None))
    facing = here + at.first
    arrived(facing)
    push(facing, second)
    plane = [here, facing, here + at.second, facing + at.second]
    for q in plane[1:]:
        odd_arrived(q)
        if q is facing:
            push_odd(q, second)
        pl.when(up)(lambda q=q: push_odd(q, above, lambda: up))
        pl.when(down)(lambda q=q: push_odd(q, below, lambda: down))

    def odd_line(d):
        low, high = at.z >= d, at.z + d < depth
        for q in plane:

            def odd_below(q=q):
                odd_arrived(q - 4 * d)
                pl.when(up)(lambda: push_odd(q - 4 * d, above, lambda: low & up))

            def odd_above(q=q):
                odd_arrived(q + 4 * d)
                pl.when(down)(lambda: push_odd(q + 4 * d, below, lambda: high & down))

            pl.when(low)(odd_below)
            pl.when(high)(odd_above)

    for d in range(1, depth):
        low, high = at.z >= d, at.z + d < depth

        def from_below(d=d, low=low):
            arrived(here - 4 * d)
            pl.when(up)(lambda: push(here - 4 * d, above, lambda: low & up))
            push(here - 4 * d, first, lambda: low)
            push(here - 4 * d, second, lambda: low)

        def from_above(d=d, high=high):
            arrived(here + 4 * d)
            pl.when(down)(lambda: push(here + 4 * d, below, lambda: high & down))
            push(here + 4 * d, first, lambda: high)
            push(here + 4 * d, second, lambda: high)

        def relay_below(d=d, low=low):
            arrived(facing - 4 * d)
            push(facing - 4 * d, second, lambda: low)

        def relay_above(d=d, high=high):
            arrived(facing + 4 * d)
            push(facing + 4 * d, second, lambda: high)

        pl.when(low)(from_below)
        pl.when(high)(from_above)
        pl.when(low)(relay_below)
        pl.when(high)(relay_above)
        if d > 1:
            odd_line(d - 1)
    if depth > 1:
        odd_line(depth - 1)
    for df in range(2):
        for d in range(depth):
            arrived(at.member(1, df, d))
    give.wait_recv()
    for n, (like, present) in enumerate(sends):

        def sent(n=n, like=like):
            remote(like, like, send_sems.at[n], misc_sems.at[0], at.sibling).wait_send()

        if present is None:
            sent()
        else:
            pl.when(present())(sent)


def gather_blocks(own_in, own_out, own_tags, tokens, cotangent, devices):
    chips = devices // 2
    depth = devices // 8
    sends = 2 * (1 + 2 + 2 + 1 + 8 * (depth - 1)) + 1 + 11 + 8 * (depth - 1)
    anywhere = pl.BlockSpec(memory_space=pl.ANY)
    return pl.pallas_call(
        functools.partial(gather_kernel, devices),
        out_shape=(
            jax.ShapeDtypeStruct((devices,) + own_in.shape, own_in.dtype),
            jax.ShapeDtypeStruct((devices,) + own_tags.shape[1:], own_tags.dtype),
            jax.ShapeDtypeStruct(tokens.shape, tokens.dtype),
        ),
        in_specs=[pl.BlockSpec(memory_space=pltpu.VMEM)] * 3 + [anywhere, anywhere],
        out_specs=(anywhere, anywhere, anywhere),
        scratch_shapes=[
            pltpu.SemaphoreType.DMA((sends,)),
            pltpu.SemaphoreType.DMA((3, chips)),
            pltpu.SemaphoreType.DMA((5,)),
        ],
        compiler_params=pltpu.CompilerParams(collective_id=0, has_side_effects=True),
        name="gather_blocks",
    )(own_in, own_out, own_tags, tokens, cotangent)


def layer_kernel(devices, per, pos, begin, tokens, cotangent, other, full, out,
                 blocks, rows, mat_a, mat_b, grads, middle, middle_got, inverse,
                 held, second_got, first_got, line_got, last_got,
                 load_sems, send_sems, second_sems, first_sems, line_sems, pair_sems):
    at = Place(devices)
    depth = at.depth
    mine = at.core
    count, width = tokens.shape
    rank = mat_a.shape[1]
    rows_k = rank // BLOCK
    rows_d = width // BLOCK
    chunks = [slice(i, i + WIDE) for i in range(0, width, WIDE)]
    sends = []

    def start(src, dst, recv, peer):
        copy = remote(src, dst, send_sems.at[len(sends)], recv, peer)
        copy.start()
        sends.append(copy)
        return copy

    def got(buf, sem):
        remote(buf, buf, send_sems.at[0], sem, at.sibling).wait_recv()

    used = full.shape[0]
    load_blocks = pltpu.make_async_copy(full, blocks.at[pl.ds(0, used)], load_sems.at[0])
    load_blocks.start()
    load_own = pltpu.make_async_copy(tokens, rows.at[pl.ds(mine * count, count)], load_sems.at[1])

    @pl.when(mine == 0)
    def _():
        load_own.start()

    @pl.when(mine == 1)
    def _():
        pltpu.make_async_copy(cotangent, rows.at[pl.ds(mine * count, count)], load_sems.at[1]).start()

    load_other = pltpu.make_async_copy(other, rows.at[pl.ds((1 - mine) * count, count)], load_sems.at[2])
    load_other.start()
    wait_peers = at.knock()
    blocks[used] = jnp.zeros((BLOCK, BLOCK), jnp.bfloat16)
    grads[rows_d * rows_k] = jnp.zeros((BLOCK, BLOCK), jnp.bfloat16)
    load_blocks.wait()

    def slot_of(b):
        return blocks[begin[b]]

    @pl.when(mine == 0)
    def _():
        def expand_a(r, carry):
            into = pl.ds(pl.multiple_of(r * BLOCK, BLOCK), BLOCK)
            for c in range(rows_k):
                mat_a[into, c * BLOCK : (c + 1) * BLOCK] = slot_of(r * rows_k + c)
            return carry

        lax.fori_loop(0, rows_d, expand_a, 0)

    @pl.when(mine == 1)
    def _():
        def expand_b(c, carry):
            into = pl.ds(pl.multiple_of(c * BLOCK, BLOCK), BLOCK)
            for r in range(rows_k):
                mat_b[r * BLOCK : (r + 1) * BLOCK, into] = slot_of(r * rows_d + c)
            return carry

        lax.fori_loop(0, rows_d, expand_b, 0)

    load_own.wait()
    load_other.wait()

    @pl.when(mine == 0)
    def _():
        total = jnp.zeros((2 * count, BLOCK), jnp.float32)
        for k in range(0, width, BLOCK):
            wide = rows[:, k : k + BLOCK].astype(jnp.float32)
            total += wide * wide
        scale = jnp.sqrt(jnp.sum(total, axis=-1, keepdims=True) / width + EPS)
        inverse[...] = jnp.broadcast_to(1.0 / scale, inverse.shape)
        pre = jnp.zeros((2 * count, rank), jnp.float32)
        for k in chunks:
            pre += jnp.dot(rows[:, k], mat_a[k, :], preferred_element_type=jnp.float32)
        middle[...] = pre * inverse[:, :1]

    @pl.when(mine == 1)
    def _():
        dact = jnp.zeros((2 * count, rank), jnp.float32)
        for k in chunks:
            dact += lax.dot_general(
                rows[:, k], mat_b[:, k], (((1,), (1,)), ((), ())), preferred_element_type=jnp.float32
            )
        middle[...] = dact

    wait_peers()
    start(middle, middle_got, pair_sems.at[0], at.sibling).wait_recv()
    across = (((0,), (0,)), ((), ()))

    @pl.when(mine == 0)
    def _():
        pre = middle[...]
        sig = jax.nn.sigmoid(pre)
        dpre = middle_got[...] * sig * (1.0 + pre * (1.0 - sig))
        dpre = (dpre * inverse[:, :1]).astype(jnp.bfloat16)
        for k in chunks:
            part = lax.dot_general(
                rows[:, k], dpre, across, preferred_element_type=jnp.float32
            ).astype(jnp.bfloat16)
            for r in range(WIDE // BLOCK):
                for c in range(rows_k):
                    grads[(k.start // BLOCK + r) * rows_k + c] = part[
                        r * BLOCK : (r + 1) * BLOCK, c * BLOCK : (c + 1) * BLOCK
                    ]

    @pl.when(mine == 1)
    def _():
        pre = middle_got[...]
        act = (pre * jax.nn.sigmoid(pre)).astype(jnp.bfloat16)
        for k in chunks:
            part = lax.dot_general(
                act, rows[:, k], across, preferred_element_type=jnp.float32
            ).astype(jnp.bfloat16)
            for r in range(rows_k):
                for c in range(WIDE // BLOCK):
                    grads[r * rows_d + k.start // BLOCK + c] = part[
                        r * BLOCK : (r + 1) * BLOCK, c * BLOCK : (c + 1) * BLOCK
                    ]

    line = sorted(range(1, depth), key=lambda d: (min(d, depth - d), d))
    dist = line[::-1] + [0]
    order = [(ds, df, d) for ds in (1, 0) for d in dist for df in (1, 0)]
    for i, (ds, df, dz) in enumerate(order):
        chip = at.member(ds, df, dz)
        parts = []
        if not ds:
            parts.append(second_got.at[df * depth + dz])
            got(parts[-1], second_sems.at[df * depth + dz])
        if not ds and not df:
            parts.append(first_got.at[dz])
            got(parts[-1], first_sems.at[dz])
            if not dz:
                for d in range(1, depth):
                    parts.append(line_got.at[d - 1])
                    got(parts[-1], line_sems.at[d - 1])

        def fill(step, carry, i=i, parts=parts, chip=chip):
            half = step // per
            part = pl.ds(pl.multiple_of((step % per) * BLOCK, BLOCK), BLOCK)
            value = grads[pos[chip * (2 * per) + step]]
            if parts:
                value = value.astype(jnp.float32)
                for q in parts:
                    value += q[half, part, :].astype(jnp.float32)
            held[i, half, part, :] = value.astype(jnp.bfloat16)
            return carry

        lax.fori_loop(0, 2 * per, fill, 0)
        if ds:
            start(held.at[i], second_got.at[df * depth + dz], second_sems.at[df * depth + dz], at.device(1, 0, 0))
        elif df:
            start(held.at[i], first_got.at[dz], first_sems.at[dz], at.device(0, 1, 0))
        elif dz:
            start(held.at[i], line_got.at[dz - 1], line_sems.at[dz - 1], at.device(0, 0, dz))
        else:
            last = start(held.at[i, 1 - mine], last_got, pair_sems.at[1], at.sibling)
            out[mine] = held[i, mine]
            last.wait_recv()
    out[1 - mine] = last_got[...]
    for copy in sends:
        copy.wait_send()


def layer_sums(places, begin, tokens, cotangent, other, full, devices, per):
    count, width = tokens.shape
    chips = devices // 2
    depth = devices // 8
    shard = (2, per * BLOCK, BLOCK)
    dma = pltpu.SemaphoreType.DMA
    vmem = pltpu.VMEM
    anywhere = pl.BlockSpec(memory_space=pl.ANY)
    scalars = pl.BlockSpec(memory_space=pltpu.SMEM)
    bf16, f32 = jnp.bfloat16, jnp.float32
    return pl.pallas_call(
        functools.partial(layer_kernel, devices, per),
        out_shape=jax.ShapeDtypeStruct(shard, bf16),
        in_specs=[scalars, scalars, anywhere, anywhere, anywhere, anywhere],
        out_specs=pl.BlockSpec(memory_space=vmem),
        scratch_shapes=[
            vmem((full.shape[0] + 1, BLOCK, BLOCK), bf16),
            vmem((2 * count, width), bf16),
            vmem((width, RANK), bf16),
            vmem((RANK, width), bf16),
            vmem((width * RANK // (BLOCK * BLOCK) + 1, BLOCK, BLOCK), bf16),
            vmem((2 * count, RANK), f32),
            vmem((2 * count, RANK), f32),
            vmem((2 * count, BLOCK), f32),
            vmem((chips,) + shard, bf16),
            vmem((2 * depth,) + shard, bf16),
            vmem((depth,) + shard, bf16),
            vmem((depth - 1,) + shard, bf16),
            vmem(shard[1:], bf16),
            dma((3,)),
            dma((chips + 1,)),
            dma((2 * depth,)),
            dma((depth,)),
            dma((depth - 1,)),
            dma((2,)),
        ],
        compiler_params=pltpu.CompilerParams(
            collective_id=1, has_side_effects=True, vmem_limit_bytes=60 * 1024 * 1024
        ),
        name="layer_sums",
    )(places, begin, tokens, cotangent, other, full)


def one_section(tokens, blocks_in, blocks_out, pos_in, pos_out, cotangent):
    devices = lax.axis_size("dp")
    per = blocks_in.shape[1]
    places = jnp.concatenate([pos_in, pos_out]).astype(jnp.bfloat16)
    places = jnp.pad(places[:, None, :], ((0, 0), (0, EXTRA - 1), (0, BLOCK - per)))
    full, tags, other = gather_blocks(blocks_in[0], blocks_out[0], places, tokens, cotangent, devices)
    count = devices * per
    slots = tags[:, 0, :per].astype(jnp.int32)
    starts = per * jnp.arange(devices)[:, None] + jnp.arange(per)[None, :]
    numbers = jnp.arange((tokens.shape[1] // BLOCK) * (RANK // BLOCK))
    found = jnp.where(slots[None] == numbers[:, None, None], starts[None], count)
    begin = jnp.min(found, axis=(1, 2)).astype(jnp.int32)
    flat = full.reshape(count, BLOCK, BLOCK)
    sums = layer_sums(slots.reshape(-1), begin, tokens, cotangent, other, flat, devices, per)
    shape = blocks_in.shape
    return (sums[0].reshape(shape), sums[1].reshape(shape))


def solution(mesh):
    in_specs = (
        P("dp", None),
        P("section", "dp", None, None),
        P("section", "dp", None, None),
        P("section", "dp"),
        P("section", "dp"),
        P("dp", None),
    )
    out_specs = (P("section", "dp", None, None), P("section", "dp", None, None))
    body = one_section if mesh.shape["section"] == 1 else per_device
    return jax.shard_map(
        body, mesh=mesh, in_specs=in_specs, out_specs=out_specs, check_vma=False
    )
```

```python
import functools

import jax
import jax.numpy as jnp
from jax import lax
from jax.experimental import pallas as pl
from jax.experimental.pallas import tpu as pltpu
from jax.sharding import PartitionSpec as P

D = 8192
RANK = 512
BLOCK = 128
MICRO = 2


EPS = 1e-05


def from_behind(block, axis, distance):
    devices = range(lax.axis_size(axis))
    route = [(i - distance, i) for i in devices if i - distance in devices]
    return lax.ppermute(block, axis, route)


def expand(blocks, places, rows_b, cols_b):
    flat = jnp.zeros((rows_b * cols_b, BLOCK, BLOCK), blocks.dtype)
    flat = flat.at[places].set(blocks, mode="drop")
    return (
        flat.reshape(rows_b, cols_b, BLOCK, BLOCK)
        .transpose(0, 2, 1, 3)
        .reshape(rows_b * BLOCK, cols_b * BLOCK)
    )


def slot_grads(left, right, places, rows_b, cols_b):
    count = left.shape[0]
    valid = places < rows_b * cols_b
    row_block = jnp.where(valid, places // cols_b, 0).astype(jnp.int32)
    col_block = jnp.where(valid, places % cols_b, 0).astype(jnp.int32)
    left_blocks = jnp.take(left.reshape(count, rows_b, BLOCK), row_block, axis=1)
    right_blocks = jnp.take(right.reshape(count, cols_b, BLOCK), col_block, axis=1)
    result = jnp.einsum(
        "tjb,tjc->jbc", left_blocks, right_blocks, preferred_element_type=jnp.float32
    )
    return jnp.where(valid[:, None, None], result, 0.0)


def norm_parts(hidden):
    wide = hidden.astype(jnp.float32)
    scale = jnp.sqrt(jnp.mean(wide * wide, axis=-1, keepdims=True) + EPS)
    return (wide, scale)


def forward_layer(hidden, mat_a, mat_b):
    wide, scale = norm_parts(hidden)
    normed = (wide / scale).astype(jnp.bfloat16)
    pre = jnp.dot(normed, mat_a, preferred_element_type=jnp.float32)
    act = (pre * jax.nn.sigmoid(pre)).astype(jnp.bfloat16)
    return (wide + jnp.dot(act, mat_b, preferred_element_type=jnp.float32)).astype(jnp.bfloat16)


def backward_layer(hidden, upstream, mat_a, mat_b):
    wide, scale = norm_parts(hidden)
    unit = wide / scale
    normed = unit.astype(jnp.bfloat16)
    pre = jnp.dot(normed, mat_a, preferred_element_type=jnp.float32)
    sig = jax.nn.sigmoid(pre)
    act = (pre * sig).astype(jnp.bfloat16)
    dact = lax.dot_general(
        upstream, mat_b, (((1,), (1,)), ((), ())), preferred_element_type=jnp.float32
    )
    dpre = (dact * sig * (1.0 + pre * (1.0 - sig))).astype(jnp.bfloat16)
    dnorm = lax.dot_general(
        dpre, mat_a, (((1,), (1,)), ((), ())), preferred_element_type=jnp.float32
    )
    inner = jnp.mean(dnorm * unit, axis=-1, keepdims=True)
    earlier = (upstream.astype(jnp.float32) + (dnorm - unit * inner) / scale).astype(jnp.bfloat16)
    return (earlier, normed, dpre, act)


def store(stack, value, picked, active):
    updated = lax.dynamic_update_slice_in_dim(stack, value[None], picked, 0)
    return jnp.where(active, updated, stack)


def per_device(tokens, blocks_in, blocks_out, pos_in, pos_out, cotangent):
    sections = lax.axis_size("section")
    here = lax.axis_index("section")
    rows_d = D // BLOCK
    rows_k = RANK // BLOCK
    full_in, full_out, all_in, all_out = (
        lax.all_gather(blocks_in, "dp", axis=1, tiled=True),
        lax.all_gather(blocks_out, "dp", axis=1, tiled=True),
        lax.all_gather(pos_in, "dp", axis=1, tiled=True),
        lax.all_gather(pos_out, "dp", axis=1, tiled=True),
    )
    mat_a = expand(full_in[0], all_in[0], rows_d, rows_k)
    mat_b = expand(full_out[0], all_out[0], rows_k, rows_d)
    micro_rows = tokens.shape[0] // MICRO
    turns = MICRO + sections - 1
    saved = jnp.zeros((MICRO, micro_rows, D), jnp.bfloat16)
    carried = jnp.zeros((micro_rows, D), jnp.bfloat16)
    for turn in range(turns):
        micro = turn - here
        active = (micro >= 0) & (micro < MICRO)
        picked = jnp.clip(micro, 0, MICRO - 1)
        first = lax.dynamic_slice_in_dim(tokens, picked * micro_rows, micro_rows, 0)
        entering = jnp.where(here == 0, first, carried)
        saved = store(saved, entering, picked, active)
        if turn < turns - 1:
            leaving = lax.cond(
                active, lambda x: forward_layer(x, mat_a, mat_b), lambda x: x, entering
            )
            carried = from_behind(leaving, "section", 1)
    kept_normed = jnp.zeros((MICRO, micro_rows, D), jnp.bfloat16)
    kept_dpre = jnp.zeros((MICRO, micro_rows, RANK), jnp.bfloat16)
    kept_act = jnp.zeros((MICRO, micro_rows, RANK), jnp.bfloat16)
    kept_upper = jnp.zeros((MICRO, micro_rows, D), jnp.bfloat16)
    carried_grad = jnp.zeros((micro_rows, D), jnp.bfloat16)
    for turn in range(turns):
        micro = turn - (sections - 1 - here)
        active = (micro >= 0) & (micro < MICRO)
        picked = jnp.clip(micro, 0, MICRO - 1)
        last = lax.dynamic_slice_in_dim(cotangent, picked * micro_rows, micro_rows, 0)
        upstream = jnp.where(here == sections - 1, last, carried_grad)
        hidden = lax.dynamic_index_in_dim(saved, picked, 0, keepdims=False)

        def run_layer():
            return backward_layer(hidden, upstream, mat_a, mat_b)

        def skip_layer():
            return (
                upstream,
                jnp.zeros((micro_rows, D), jnp.bfloat16),
                jnp.zeros((micro_rows, RANK), jnp.bfloat16),
                jnp.zeros((micro_rows, RANK), jnp.bfloat16),
            )

        earlier, normed, dpre, act = lax.cond(active, run_layer, skip_layer)
        kept_normed = store(kept_normed, normed, picked, active)
        kept_dpre = store(kept_dpre, dpre, picked, active)
        kept_act = store(kept_act, act, picked, active)
        kept_upper = store(kept_upper, upstream, picked, active)
        if turn < turns - 1:
            carried_grad = from_behind(earlier, "section", -1)
    all_rows = MICRO * micro_rows
    terms_in = slot_grads(
        kept_normed.reshape(all_rows, D),
        kept_dpre.reshape(all_rows, RANK),
        all_in[0],
        rows_d,
        rows_k,
    )[None]
    terms_out = slot_grads(
        kept_act.reshape(all_rows, RANK),
        kept_upper.reshape(all_rows, D),
        all_out[0],
        rows_k,
        rows_d,
    )[None]
    sums_in, sums_out = (
        lax.psum_scatter(
            terms_in.astype(jnp.bfloat16), "dp", scatter_dimension=1, tiled=True
        ).astype(jnp.float32),
        lax.psum_scatter(
            terms_out.astype(jnp.bfloat16), "dp", scatter_dimension=1, tiled=True
        ).astype(jnp.float32),
    )
    return (sums_in.astype(jnp.bfloat16), sums_out.astype(jnp.bfloat16))


EXTRA= 16
WIDE = 1024


class Place:
    def __init__(self, devices):
        me = lax.axis_index("dp")
        self.depth = devices // 8
        self.me = me
        self.core = me % 2
        self.chip = me // 2
        x = self.chip % 2
        y = (self.chip // 2) % 2
        self.z = self.chip // 4
        dx = 1 - 2 * x
        dy = 2 * (1 - 2 * y)
        self.first = (1 - self.core) * dx + self.core * dy
        self.second = (1 - self.core) * dy + self.core * dx
        self.sibling = me + 1 - 2 * self.core

    def member(self, ds, df, dz, first=None, second=None):
        first = self.first if first is None else first
        second = self.second if second is None else second
        along = ((self.z + dz) % self.depth - self.z) * 4
        return self.chip + along + df * first + ds * second

    def device(self, ds, df, dz):
        return 2 * self.member(ds, df, dz) + self.core

    def knock(self):
        peers = [self.sibling, self.device(1, 0, 0), self.device(0, 1, 0)]
        peers += [self.device(0, 0, d) for d in range(1, self.depth)]
        barrier = pltpu.get_barrier_semaphore()
        for peer in peers:
            pl.semaphore_signal(
                barrier, inc=1, device_id={"dp": peer}, device_id_type=pl.DeviceIdType.MESH
            )
        return lambda: pl.semaphore_wait(barrier, len(peers))


def remote(src, dst, send, recv, peer):
    return pltpu.make_async_remote_copy(
        src_ref=src,
        dst_ref=dst,
        send_sem=send,
        recv_sem=recv,
        device_id={"dp": peer},
        device_id_type=pl.DeviceIdType.MESH,
    )


def gather_kernel(
    devices, own_in, own_out, own_tags, tokens, cotangent, full, tags, other, send_sems, chip_sems, misc_sems
):
    at = Place(devices)
    depth = at.depth
    mine = at.core
    sends = []

    def on_core(core):
        return pl.when(mine == core)

    def local_copy(source):
        return pltpu.make_async_copy(source, full.at[at.me], misc_sems.at[0])

    on_core(0)(lambda: local_copy(own_in).start())
    on_core(1)(lambda: local_copy(own_out).start())
    local = [
        local_copy(own_in),
        pltpu.make_async_copy(own_tags.at[mine], tags.at[at.me], misc_sems.at[3]),
    ]
    local[1].start()
    at.knock()()

    def start(src, dst, recv, peer, like, present=None):
        remote(src, dst, send_sems.at[len(sends)], recv, peer).start()
        sends.append((like, present))

    def pair_copy(source):
        return remote(source, full.at[at.me], send_sems.at[0], misc_sems.at[1], at.sibling)

    on_core(0)(lambda: pair_copy(own_out).start())
    on_core(1)(lambda: pair_copy(own_in).start())
    sends.append((own_in, None))
    start(own_tags.at[1 - mine], tags.at[at.me], misc_sems.at[4], at.sibling, own_tags.at[0])
    pair = [
        pair_copy(own_in),
        remote(own_tags.at[0], tags.at[at.me], send_sems.at[0], misc_sems.at[4], at.sibling),
    ]

    per = own_in.shape[0]
    bulk = full.at[pl.ds(0, 2), pl.ds(0, per - 1)]
    spare = full.at[pl.ds(0, 2), pl.ds(per - 1, 1)]

    def odd(chip):
        return full.at[pl.ds(2 * chip, 2), pl.ds(per - 1, 1)]

    def push_odd(chip, peer, present=None):
        start(odd(chip), odd(chip), chip_sems.at[2, chip], peer, spare, present)

    def odd_arrived(chip):
        remote(odd(chip), odd(chip), send_sems.at[0], chip_sems.at[2, chip], at.sibling).wait_recv()

    def shards(chip):
        return (
            (full.at[pl.ds(2 * chip, 2), pl.ds(0, per - 1)], chip_sems.at[0, chip]),
            (tags.at[pl.ds(2 * chip, 2)], chip_sems.at[1, chip]),
        )

    def push(chip, peer, present=None):
        for (shard, sem), like in zip(shards(chip), (bulk, tags.at[pl.ds(0, 2)])):
            start(shard, shard, sem, peer, like, present)

    def arrived(chip):
        for shard, sem in shards(chip):
            remote(shard, shard, send_sems.at[0], sem, at.sibling).wait_recv()

    first, second = at.device(0, 1, 0), at.device(1, 0, 0)
    above, below = at.me + 8, at.me - 8
    up, down = at.z + 1 < depth, at.z >= 1
    for copy in local:
        copy.wait()
    for copy in pair:
        copy.wait_recv()
    here = at.chip
    pl.when(up)(lambda: push(here, above, lambda: up))
    pl.when(down)(lambda: push(here, below, lambda: down))
    push(here, second)
    push(here, first)
    push_odd(here, first)
    push_odd(here, second)
    pl.when(up)(lambda: push_odd(here, above, lambda: up))
    pl.when(down)(lambda: push_odd(here, below, lambda: down))
    swap = misc_sems.at[2]
    give = remote(tokens, other, send_sems.at[len(sends)], swap, at.sibling)
    keep = remote(cotangent, other, send_sems.at[len(sends)], swap, at.sibling)
    on_core(0)(lambda: keep.start())
    on_core(1)(lambda: give.start())
    sends.append((tokens, None))
    facing = here + at.first
    arrived(facing)
    push(facing, second)
    plane = [here, facing, here + at.second, facing + at.second]
    for q in plane[1:]:
        odd_arrived(q)
        if q is facing:
            push_odd(q, second)
        pl.when(up)(lambda q=q: push_odd(q, above, lambda: up))
        pl.when(down)(lambda q=q: push_odd(q, below, lambda: down))

    def odd_line(d):
        low, high = at.z >= d, at.z + d < depth
        for q in plane:

            def odd_below(q=q):
                odd_arrived(q - 4 * d)
                pl.when(up)(lambda: push_odd(q - 4 * d, above, lambda: low & up))

            def odd_above(q=q):
                odd_arrived(q + 4 * d)
                pl.when(down)(lambda: push_odd(q + 4 * d, below, lambda: high & down))

            pl.when(low)(odd_below)
            pl.when(high)(odd_above)

    for d in range(1, depth):
        low, high = at.z >= d, at.z + d < depth

        def from_below(d=d, low=low):
            arrived(here - 4 * d)
            pl.when(up)(lambda: push(here - 4 * d, above, lambda: low & up))
            push(here - 4 * d, first, lambda: low)
            push(here - 4 * d, second, lambda: low)

        def from_above(d=d, high=high):
            arrived(here + 4 * d)
            pl.when(down)(lambda: push(here + 4 * d, below, lambda: high & down))
            push(here + 4 * d, first, lambda: high)
            push(here + 4 * d, second, lambda: high)

        def relay_below(d=d, low=low):
            arrived(facing - 4 * d)
            push(facing - 4 * d, second, lambda: low)

        def relay_above(d=d, high=high):
            arrived(facing + 4 * d)
            push(facing + 4 * d, second, lambda: high)

        pl.when(low)(from_below)
        pl.when(high)(from_above)
        pl.when(low)(relay_below)
        pl.when(high)(relay_above)
        if d > 1:
            odd_line(d - 1)
    if depth > 1:
        odd_line(depth - 1)
    for df in range(2):
        for d in range(depth):
            arrived(at.member(1, df, d))
    give.wait_recv()
    for n, (like, present) in enumerate(sends):

        def sent(n=n, like=like):
            remote(like, like, send_sems.at[n], misc_sems.at[0], at.sibling).wait_send()

        if present is None:
            sent()
        else:
            pl.when(present())(sent)


def gather_blocks(own_in, own_out, own_tags, tokens, cotangent, devices):
    chips = devices // 2
    depth = devices // 8
    sends = 2 * (1 + 2 + 2 + 1 + 8 * (depth - 1)) + 1 + 11 + 8 * (depth - 1)
    anywhere = pl.BlockSpec(memory_space=pl.ANY)
    return pl.pallas_call(
        functools.partial(gather_kernel, devices),
        out_shape=(
            jax.ShapeDtypeStruct((devices,) + own_in.shape, own_in.dtype),
            jax.ShapeDtypeStruct((devices,) + own_tags.shape[1:], own_tags.dtype),
            jax.ShapeDtypeStruct(tokens.shape, tokens.dtype),
        ),
        in_specs=[pl.BlockSpec(memory_space=pltpu.VMEM)] * 3 + [anywhere, anywhere],
        out_specs=(anywhere, anywhere, anywhere),
        scratch_shapes=[
            pltpu.SemaphoreType.DMA((sends,)),
            pltpu.SemaphoreType.DMA((3, chips)),
            pltpu.SemaphoreType.DMA((5,)),
        ],
        compiler_params=pltpu.CompilerParams(collective_id=0, has_side_effects=True),
        name="gather_blocks",
    )(own_in, own_out, own_tags, tokens, cotangent)


def layer_kernel(devices, per, pos, begin, tokens, cotangent, other, full, out,
                 blocks, rows, mat_a, mat_b, grads, middle, packed, middle_got, inverse,
                 held, second_got, first_got, line_got, last_got,
                 load_sems, send_sems, second_sems, first_sems, line_sems, pair_sems):
    at = Place(devices)
    depth = at.depth
    mine = at.core
    count, width = tokens.shape
    rank = mat_a.shape[1]
    rows_k = rank // BLOCK
    rows_d = width // BLOCK
    chunks = [slice(i, i + WIDE) for i in range(0, width, WIDE)]
    sends = []

    def start(src, dst, recv, peer):
        copy = remote(src, dst, send_sems.at[len(sends)], recv, peer)
        copy.start()
        sends.append(copy)
        return copy

    def got(buf, sem):
        remote(buf, buf, send_sems.at[0], sem, at.sibling).wait_recv()

    used = full.shape[0]
    load_blocks = pltpu.make_async_copy(full, blocks.at[pl.ds(0, used)], load_sems.at[0])
    load_blocks.start()
    load_own = pltpu.make_async_copy(tokens, rows.at[pl.ds(mine * count, count)], load_sems.at[1])

    @pl.when(mine == 0)
    def _():
        load_own.start()

    @pl.when(mine == 1)
    def _():
        pltpu.make_async_copy(cotangent, rows.at[pl.ds(mine * count, count)], load_sems.at[1]).start()

    load_other = pltpu.make_async_copy(other, rows.at[pl.ds((1 - mine) * count, count)], load_sems.at[2])
    load_other.start()
    wait_peers = at.knock()
    blocks[used] = jnp.zeros((BLOCK, BLOCK), jnp.bfloat16)
    grads[rows_d * rows_k] = jnp.zeros((BLOCK, BLOCK), jnp.bfloat16)
    load_blocks.wait()

    def slot_of(b):
        return blocks[begin[b]]

    @pl.when(mine == 0)
    def _():
        def expand_a(r, carry):
            into = pl.ds(pl.multiple_of(r * BLOCK, BLOCK), BLOCK)
            for c in range(rows_k):
                mat_a[into, c * BLOCK : (c + 1) * BLOCK] = slot_of(r * rows_k + c)
            return carry

        lax.fori_loop(0, rows_d, expand_a, 0)

    @pl.when(mine == 1)
    def _():
        def expand_b(c, carry):
            into = pl.ds(pl.multiple_of(c * BLOCK, BLOCK), BLOCK)
            for r in range(rows_k):
                mat_b[r * BLOCK : (r + 1) * BLOCK, into] = slot_of(r * rows_d + c)
            return carry

        lax.fori_loop(0, rows_d, expand_b, 0)

    load_own.wait()
    load_other.wait()

    @pl.when(mine == 0)
    def _():
        total = jnp.zeros((2 * count, BLOCK), jnp.float32)
        for k in range(0, width, BLOCK):
            wide = rows[:, k : k + BLOCK].astype(jnp.float32)
            total += wide * wide
        scale = jnp.sqrt(jnp.sum(total, axis=-1, keepdims=True) / width + EPS)
        inverse[...] = jnp.broadcast_to(1.0 / scale, inverse.shape)
        pre = jnp.zeros((2 * count, rank), jnp.float32)
        for k in chunks:
            pre += jnp.dot(rows[:, k], mat_a[k, :], preferred_element_type=jnp.float32)
        middle[...] = pre * inverse[:, :1]

    @pl.when(mine == 1)
    def _():
        dact = jnp.zeros((2 * count, rank), jnp.float32)
        for k in chunks:
            dact += lax.dot_general(
                rows[:, k], mat_b[:, k], (((1,), (1,)), ((), ())), preferred_element_type=jnp.float32
            )
        middle[...] = dact

    wait_peers()
    packed[...] = middle[...].astype(jnp.bfloat16)
    start(packed, middle_got, pair_sems.at[0], at.sibling).wait_recv()
    across = (((0,), (0,)), ((), ()))

    @pl.when(mine == 0)
    def _():
        pre = middle[...]
        sig = jax.nn.sigmoid(pre)
        dpre = middle_got[...].astype(jnp.float32) * sig * (1.0 + pre * (1.0 - sig))
        dpre = (dpre * inverse[:, :1]).astype(jnp.bfloat16)
        for k in chunks:
            part = lax.dot_general(
                rows[:, k], dpre, across, preferred_element_type=jnp.float32
            ).astype(jnp.bfloat16)
            for r in range(WIDE // BLOCK):
                for c in range(rows_k):
                    grads[(k.start // BLOCK + r) * rows_k + c] = part[
                        r * BLOCK : (r + 1) * BLOCK, c * BLOCK : (c + 1) * BLOCK
                    ]

    @pl.when(mine == 1)
    def _():
        pre = middle_got[...].astype(jnp.float32)
        act = (pre * jax.nn.sigmoid(pre)).astype(jnp.bfloat16)
        for k in chunks:
            part = lax.dot_general(
                act, rows[:, k], across, preferred_element_type=jnp.float32
            ).astype(jnp.bfloat16)
            for r in range(rows_k):
                for c in range(WIDE // BLOCK):
                    grads[r * rows_d + k.start // BLOCK + c] = part[
                        r * BLOCK : (r + 1) * BLOCK, c * BLOCK : (c + 1) * BLOCK
                    ]

    line = sorted(range(1, depth), key=lambda d: (min(d, depth - d), d))
    dist = line[::-1] + [0]
    order = [(ds, df, d) for ds in (1, 0) for d in dist for df in (1, 0)]
    for i, (ds, df, dz) in enumerate(order):
        chip = at.member(ds, df, dz)
        parts = []
        if not ds:
            parts.append(second_got.at[df * depth + dz])
            got(parts[-1], second_sems.at[df * depth + dz])
        if not ds and not df:
            parts.append(first_got.at[dz])
            got(parts[-1], first_sems.at[dz])
            if not dz:
                for d in range(1, depth):
                    parts.append(line_got.at[d - 1])
                    got(parts[-1], line_sems.at[d - 1])

        def fill(step, carry, i=i, parts=parts, chip=chip):
            half = step // per
            part = pl.ds(pl.multiple_of((step % per) * BLOCK, BLOCK), BLOCK)
            value = grads[pos[chip * (2 * per) + step]]
            if parts:
                value = value.astype(jnp.float32)
                for q in parts:
                    value += q[half, part, :].astype(jnp.float32)
            held[i, half, part, :] = value.astype(jnp.bfloat16)
            return carry

        lax.fori_loop(0, 2 * per, fill, 0)
        if ds:
            start(held.at[i], second_got.at[df * depth + dz], second_sems.at[df * depth + dz], at.device(1, 0, 0))
        elif df:
            start(held.at[i], first_got.at[dz], first_sems.at[dz], at.device(0, 1, 0))
        elif dz:
            start(held.at[i], line_got.at[dz - 1], line_sems.at[dz - 1], at.device(0, 0, dz))
        else:
            last = start(held.at[i, 1 - mine], last_got, pair_sems.at[1], at.sibling)
            out[mine] = held[i, mine]
            last.wait_recv()
    out[1 - mine] = last_got[...]
    for copy in sends:
        copy.wait_send()


def layer_sums(places, begin, tokens, cotangent, other, full, devices, per):
    count, width = tokens.shape
    chips = devices // 2
    depth = devices // 8
    shard = (2, per * BLOCK, BLOCK)
    dma = pltpu.SemaphoreType.DMA
    vmem = pltpu.VMEM
    anywhere = pl.BlockSpec(memory_space=pl.ANY)
    scalars = pl.BlockSpec(memory_space=pltpu.SMEM)
    bf16, f32 = jnp.bfloat16, jnp.float32
    return pl.pallas_call(
        functools.partial(layer_kernel, devices, per),
        out_shape=jax.ShapeDtypeStruct(shard, bf16),
        in_specs=[scalars, scalars, anywhere, anywhere, anywhere, anywhere],
        out_specs=pl.BlockSpec(memory_space=vmem),
        scratch_shapes=[
            vmem((full.shape[0] + 1, BLOCK, BLOCK), bf16),
            vmem((2 * count, width), bf16),
            vmem((width, RANK), bf16),
            vmem((RANK, width), bf16),
            vmem((width * RANK // (BLOCK * BLOCK) + 1, BLOCK, BLOCK), bf16),
            vmem((2 * count, RANK), f32),
            vmem((2 * count, RANK), bf16),
            vmem((2 * count, RANK), bf16),
            vmem((2 * count, BLOCK), f32),
            vmem((chips,) + shard, bf16),
            vmem((2 * depth,) + shard, bf16),
            vmem((depth,) + shard, bf16),
            vmem((depth - 1,) + shard, bf16),
            vmem(shard[1:], bf16),
            dma((3,)),
            dma((chips + 1,)),
            dma((2 * depth,)),
            dma((depth,)),
            dma((depth - 1,)),
            dma((2,)),
        ],
        compiler_params=pltpu.CompilerParams(
            collective_id=1, has_side_effects=True, vmem_limit_bytes=60 * 1024 * 1024
        ),
        name="layer_sums",
    )(places, begin, tokens, cotangent, other, full)


def one_section(tokens, blocks_in, blocks_out, pos_in, pos_out, cotangent):
    devices = lax.axis_size("dp")
    per = blocks_in.shape[1]
    places = jnp.concatenate([pos_in, pos_out]).astype(jnp.bfloat16)
    places = jnp.pad(places[:, None, :], ((0, 0), (0, EXTRA - 1), (0, BLOCK - per)))
    full, tags, other = gather_blocks(blocks_in[0], blocks_out[0], places, tokens, cotangent, devices)
    count = devices * per
    slots = tags[:, 0, :per].astype(jnp.int32)
    starts = per * jnp.arange(devices)[:, None] + jnp.arange(per)[None, :]
    numbers = jnp.arange((tokens.shape[1] // BLOCK) * (RANK // BLOCK))
    found = jnp.where(slots[None] == numbers[:, None, None], starts[None], count)
    begin = jnp.min(found, axis=(1, 2)).astype(jnp.int32)
    flat = full.reshape(count, BLOCK, BLOCK)
    sums = layer_sums(slots.reshape(-1), begin, tokens, cotangent, other, flat, devices, per)
    shape = blocks_in.shape
    return (sums[0].reshape(shape), sums[1].reshape(shape))


def solution(mesh):
    in_specs = (
        P("dp", None),
        P("section", "dp", None, None),
        P("section", "dp", None, None),
        P("section", "dp"),
        P("section", "dp"),
        P("dp", None),
    )
    out_specs = (P("section", "dp", None, None), P("section", "dp", None, None))
    body = one_section if mesh.shape["section"] == 1 else per_device
    return jax.shard_map(
        body, mesh=mesh, in_specs=in_specs, out_specs=out_specs, check_vma=False
    )
```
